128 devices in a mesh: gx: 16 (over y, x), gy: 4 (over z), gz: 2 (over core).
Axes of the slice: x: 4, y: 4, z: 4, core: 2. Of those that a mesh axis runs over, the one named last changes fastest.
Arguments:
- adjoint: float32 [5, 384, 64, 256], P(None, 'gx', 'gy', 'gz'), may hold values from -6 to 6
- base_density: float32 [384, 64, 256], P('gx', 'gy', 'gz'), may hold values from 0.5 to 2
- base_velocity: float32 [3, 384, 64, 256], P(None, 'gx', 'gy', 'gz'), may hold values from -2.5 to 2.5
- base_pressure: float32 [384, 64, 256], P('gx', 'gy', 'gz'), may hold values from 0.5 to 2
Outputs:
- tendency: float32 [5, 384, 64, 256], P(None, 'gx', 'gy', 'gz')
- updated: float32 [5, 384, 64, 256], P(None, 'gx', 'gy', 'gz')
The draws below stay inside these ranges and needn't reach their ends.
All inputs are finite; a program needn't handle non-finite values.
Results may differ from the reference program's by a relative error of at most 0.0003.
Values sent between devices are 32-bit elements; how exact they have to be, the bound alone decides.
A program may use at most 192 MiB of HBM per device.

```python
import math
import jax
import jax.numpy as jnp
from jax import lax

VARIABLES = 5
NX = 384
NY = 64
NZ = 256


def draw_adjoint(key, part):
    key_rough = jax.random.fold_in(key, 11)
    shape_all = (VARIABLES, NX, NY, NZ)
    return jnp.clip(jax.random.normal(key_rough, shape_all, jnp.float32), -6.0, 6.0)


def draw_base_velocity(key, part):
    key_speed = jax.random.fold_in(key, 37)
    shape_all = (3, NX, NY, NZ)
    return jnp.clip(0.5 * jax.random.normal(key_speed, shape_all, jnp.float32), -2.5, 2.5)


def level_of(rng, dims, split, smallest, high):
    gain = 1.0
    for dim, shards_of in split:
        draws = jax.random.uniform(jax.random.fold_in(jax.random.fold_in(rng, 6), dim), (shards_of,), jnp.float32, smallest / len(split), high / len(split))
        gain = gain * jnp.repeat(jnp.exp(draws), dims[dim] // shards_of).reshape((-1,) + (1,) * (len(dims) - 1 - dim))
    return gain


def setup_inputs(seed: int = 0) -> dict:
    seeds = jax.random.split(jax.random.key(seed), 5)
    return {
        "adjoint": draw_adjoint(jax.random.fold_in(seeds[4], 71), 0),
        "base_density": jnp.clip(jnp.exp(math.log(2.0) - 1.3862944 * jax.random.uniform(seeds[1], (NX, NY, NZ), jnp.float32) ** level_of(seeds[1], (NX, NY, NZ), ((0, 16), (1, 4), (2, 2)), -0.2, 0.2)), 0.5, 2.0),
        "base_velocity": draw_base_velocity(jax.random.fold_in(seeds[4], 71), 0),
        "base_pressure": jnp.clip(jnp.exp(math.log(2.0) - 1.3862944 * jax.random.uniform(seeds[3], (NX, NY, NZ), jnp.float32) ** level_of(seeds[3], (NX, NY, NZ), ((0, 16), (1, 4), (2, 2)), -0.2, 0.2)), 0.5, 2.0),
    }


GAMMA_GAS = 1.4
RATIO = 1.0 / 3.0
COEF_NEAR = 7.0 / 9.0
COEF_FAR = 1.0 / 36.0
NU_COEF = 0.5
STEP_COEF = 0.5
HIGHEST = lax.Precision.HIGHEST

def conserved(density, velocity, pressure):
    momentum = density[None] * velocity
    energy = pressure / (GAMMA_GAS - 1.0) + 0.5 * density * lax.optimization_barrier(jnp.sum(velocity * velocity, axis=0))
    return jnp.concatenate([density[None], momentum, energy[None]], axis=0)

def fluxes(state_in):
    density = state_in[0]
    momentum = state_in[1:4]
    energy = state_in[4]
    velocity = momentum / density[None]
    pressure = (GAMMA_GAS - 1.0) * (energy - 0.5 * lax.optimization_barrier(jnp.sum(momentum * velocity, axis=0)))
    result = []
    for direction in range(3):
        speed_dir = velocity[direction]
        entries = [momentum[direction]]
        for component in range(3):
            summand = momentum[component] * speed_dir
            if component == direction:
                summand = summand + pressure
            entries.append(summand)
        entries.append((energy + pressure) * speed_dir)
        result.append(jnp.stack(entries, axis=0))
    return tuple(result)

def transposed_derivative(total, periodic):
    identity_mat = jnp.eye(total, dtype=jnp.float32)
    if periodic:
        upper_one = jnp.roll(identity_mat, 1, axis=1)
        lower_one = jnp.roll(identity_mat, -1, axis=1)
        upper_two = jnp.roll(identity_mat, 2, axis=1)
        lower_two = jnp.roll(identity_mat, -2, axis=1)
    else:
        upper_one = jnp.eye(total, k=1, dtype=jnp.float32)
        lower_one = jnp.eye(total, k=-1, dtype=jnp.float32)
        upper_two = jnp.eye(total, k=2, dtype=jnp.float32)
        lower_two = jnp.eye(total, k=-2, dtype=jnp.float32)
    banded = identity_mat + RATIO * (upper_one + lower_one)
    stencil_mat = COEF_NEAR * (upper_one - lower_one) + COEF_FAR * (upper_two - lower_two)
    return -jnp.dot(stencil_mat, jnp.linalg.inv(banded), precision=HIGHEST)

def along_axis(matrix, field_in, axis_at):
    product = jnp.tensordot(matrix, field_in, axes=((1,), (axis_at,)), precision=HIGHEST)
    return jnp.moveaxis(product, 0, axis_at)

def reference(adjoint, base_density, base_velocity, base_pressure):
    base_state = conserved(base_density, base_velocity, base_pressure)
    operators = [transposed_derivative(NX, False), transposed_derivative(NY, False), transposed_derivative(NZ, True)]
    firsts = tuple((along_axis(operators[number], adjoint, number + 1) for number in range(3)))
    outputs, pullback = jax.vjp(fluxes, base_state)
    convective = pullback(firsts)[0]
    viscous = along_axis(operators[0], firsts[0], 1) + along_axis(operators[1], firsts[1], 2) + along_axis(operators[2], firsts[2], 3)
    tendency = NU_COEF * viscous - convective
    updated = adjoint + STEP_COEF * tendency
    return (tendency, updated)
```

```python
import functools

import jax
import jax.numpy as jnp
import numpy as np
from jax import lax
from jax.experimental import pallas as pl
from jax.experimental.pallas import tpu as pltpu
from jax.sharding import PartitionSpec as P

GAMMA_LESS = 0.4
RATIO = 1.0 / 3.0
COEF_NEAR = 7.0 / 9.0
COEF_FAR = 1.0 / 36.0
RANK = 4
F32 = jnp.float32
BF16 = jnp.bfloat16


def derivative(total, periodic):
    eye = np.eye(total)
    if periodic:
        up1, lo1, up2, lo2 = (np.roll(eye, s, axis=1) for s in (1, -1, 2, -2))
    else:
        up1, lo1, up2, lo2 = (np.eye(total, k=s) for s in (1, -1, 2, -2))
    banded = eye + RATIO * (up1 + lo1)
    stencil = COEF_NEAR * (up1 - lo1) + COEF_FAR * (up2 - lo2)
    return -stencil @ np.linalg.inv(banded)


def stacked(matrix, rows, cols):
    return np.vstack([matrix[rows, cols], (matrix @ matrix)[rows, cols]])


def line_factors(block):
    long = derivative(9 * block, False)
    near = derivative(4 * block, False)
    own = slice(4 * block, 5 * block)
    local = stacked(long, own, own)
    sides = []
    for beside, edge in (
        (slice(3 * block, 4 * block), slice(0, block)),
        (slice(5 * block, 6 * block), slice(3 * block, 4 * block)),
    ):
        basis, size, functional = np.linalg.svd(stacked(long, own, beside))
        basis = basis[:, :RANK]
        sides.append(
            (basis, size[:RANK, None] * functional[:RANK], basis.T @ (stacked(near, edge, edge) - local))
        )
    return local, sides


def high_low(matrix, axis):
    high = matrix.astype(np.float32).astype(BF16)
    low = (matrix - high.astype(np.float64)).astype(np.float32).astype(BF16)
    return np.concatenate([high, low], axis=axis)


@functools.lru_cache(maxsize=None)
def tables(nx, ny, nz, cx):
    loc_x, side_x = line_factors(nx)
    loc_y, side_y = line_factors(ny)
    eye_x, eye_y, eye_c = np.eye(nx), np.eye(ny), np.eye(cx)
    local = np.stack(
        [
            high_low(m, 0)
            for m in (
                np.kron(loc_x[nx:], eye_y) + np.kron(eye_x, loc_y[ny:]),
                np.kron(loc_x[:nx], eye_y),
                np.kron(eye_x, loc_y[:ny]),
            )
        ]
    )
    state_y = np.stack(
        [
            np.stack([high_low(np.kron(eye_c, m), 0) for m in pair])
            for pair in ((side_y[1][1], side_y[0][2]), (side_y[0][1], side_y[1][2]))
        ]
    )
    state_x = np.stack(
        [
            np.stack([high_low(np.kron(m, eye_y), 0) for m in pair])
            for pair in ((side_x[1][1], side_x[0][2]), (side_x[0][1], side_x[1][2]))
        ]
    )
    correct = []
    for c in range(nx // cx):
        rows = slice(c * cx, (c + 1) * cx)
        of_y = [np.kron(eye_c, s[0][ny:]) for s in side_y], [np.kron(eye_c, s[0][:ny]) for s in side_y]
        of_x = (
            [np.kron(s[0][nx:][rows], eye_y) for s in side_x],
            [np.kron(s[0][:nx][rows], eye_y) for s in side_x],
        )
        none_y, none_x = [np.zeros_like(m) for m in of_y[0]], [np.zeros_like(m) for m in of_x[0]]
        whole = np.vstack(
            [
                np.hstack(of_y[0] + of_x[0]),
                np.hstack(none_y + of_x[1]),
                np.hstack(of_y[1] + none_x),
            ]
        )
        whole = np.hstack([whole, np.zeros((whole.shape[0], 256 - whole.shape[1]))])
        correct.append(high_low(whole, 0))
    span = derivative(2 * nz, True)
    both = np.hstack([span[:nz].T, (span @ span)[:nz].T])
    return local, state_y, state_x, np.stack(correct), high_low(both, 1)


def split(value):
    high = value.astype(BF16)
    low = (value - high.astype(F32)).astype(BF16)
    return high, low


def product(matrix, columns):
    full = jnp.dot(matrix, columns, preferred_element_type=F32)
    rows = full.shape[0] // 2
    return full[:rows, :128] + full[:rows, 128:] + full[rows:, :128]


def kernel(
    cx, counts,
    adj_hbm, rho_hbm, vel_hbm, pre_hbm, loc_hbm, sty_hbm, stx_hbm, cor_hbm, spn_hbm,
    out_hbm,
    adj, rho, vel, pre, loc, sty, stx, cor, spn,
    cols, other, ysend, yrecv, xsend, xrecv, twice, fx, fy, fz, out,
    in_sem, out_sem, ys_sem, yr_sem, xs_sem, xr_sem, zs_sem, zr_sem,
):
    gx, gy, gz = (lax.axis_index(n) for n in ("gx", "gy", "gz"))
    n_gx, n_gy = counts
    variables = adj.shape[0]
    rows_c = cx * 16
    chunks = adj.shape[1] // rows_c

    loads = [
        pltpu.make_async_copy(src, dst, in_sem.at[k])
        for k, (src, dst) in enumerate(
            ((adj_hbm, adj), (sty_hbm, sty), (stx_hbm, stx), (loc_hbm, loc), (spn_hbm, spn),
             (rho_hbm, rho), (vel_hbm, vel), (pre_hbm, pre), (cor_hbm, cor))
        )
    ]
    for load in loads:
        load.start()

    has = (gx > 0, gx < n_gx - 1, gy > 0, gy < n_gy - 1)
    to = ({"gx": gx - 1}, {"gx": gx + 1}, {"gy": gy - 1}, {"gy": gy + 1})
    partner = {"gz": 1 - gz}
    barrier = pltpu.get_barrier_semaphore()
    for there, where in zip(has, to):

        @pl.when(there)
        def _(where=where):
            pl.semaphore_signal(barrier, inc=1, device_id=where, device_id_type=pl.DeviceIdType.MESH)

    pl.semaphore_signal(barrier, inc=1, device_id=partner, device_id_type=pl.DeviceIdType.MESH)

    def remote(src, dst, send, recv, where):
        return pltpu.make_async_remote_copy(
            src_ref=src, dst_ref=dst, send_sem=send, recv_sem=recv,
            device_id=where, device_id_type=pl.DeviceIdType.MESH,
        )

    def y_copy(slot, c):
        return remote(
            ysend.at[slot, c], yrecv.at[1 - slot, c], ys_sem.at[slot, c], yr_sem.at[1 - slot, c], to[2 + slot]
        )

    def x_copy(slot):
        return remote(xsend.at[slot], xrecv.at[1 - slot], xs_sem.at[slot], xr_sem.at[1 - slot], to[slot])

    def z_copy(v):
        return remote(adj_hbm.at[v], other.at[v], zs_sem.at[v], zr_sem.at[v], partner)

    loads[0].wait()
    for v in range(variables):
        high, low = split(adj[v])
        cols[v, :, :128] = high
        cols[v, :, 128:] = low

    edge = tuple(jnp.where(there, 0, 1) for there in has)
    loads[1].wait()
    neighbours = sum(jnp.where(there, 1, 0) for there in has) + 1
    for c in range(chunks):

        for v in range(variables):
            block = cols[v, c * rows_c : (c + 1) * rows_c, :]
            for slot in range(2):
                ysend[slot, c, v] = product(sty[slot, edge[2 + slot]], block)
        if c == 0:
            pl.semaphore_wait(barrier, neighbours)
        for slot in range(2):

            @pl.when(has[2 + slot])
            def _(slot=slot):
                y_copy(slot, c).start()

            @pl.when(jnp.logical_not(has[2 + slot]))
            def _(slot=slot):
                yrecv[slot, c] = ysend[slot, c]

    loads[2].wait()

    @pl.loop(0, variables)
    def _(v):
        for slot in range(2):
            xsend[slot, v] = product(stx[slot, edge[slot]], cols[v])

    for slot in range(2):

        @pl.when(has[slot])
        def _(slot=slot):
            x_copy(slot).start()

        @pl.when(jnp.logical_not(has[slot]))
        def _(slot=slot):
            xrecv[slot] = xsend[slot]

    for v in range(variables):
        z_copy(v).start()

    loads[3].wait()

    @pl.loop(0, variables)
    def _(v):
        for kind, into in enumerate((twice, fx, fy)):
            into[v] = product(loc[kind], cols[v])

    loads[4].wait()
    for v in range(variables):
        z_copy(v).wait_recv()

    @pl.loop(0, variables)
    def _(v):
        high, low = split(other[v])
        high = jnp.concatenate([cols[v, :, :128], high], axis=1)
        low = jnp.concatenate([cols[v, :, 128:], low], axis=1)
        width = spn.shape[1] // 2
        full = (
            jnp.dot(high, spn[:, :width], preferred_element_type=F32)
            + jnp.dot(low, spn[:, :width], preferred_element_type=F32)
            + jnp.dot(high, spn[:, width:], preferred_element_type=F32)
        )
        fz[v] = full[:, :128]
        twice[v] += full[:, 128:]

    for load in loads[5:]:
        load.wait()
    for slot in range(2):

        @pl.when(has[slot])
        def _(slot=slot):
            x_copy(1 - slot).wait_recv()

    zeros = jnp.zeros((256 - 2 * RANK * (cx + 16), 128), F32)
    writes = []
    for c in range(chunks):
        rows = pl.ds(c * rows_c, rows_c)
        for slot in range(2):

            @pl.when(has[2 + slot])
            def _(slot=slot):
                y_copy(1 - slot, c).wait_recv()

        @pl.loop(0, variables)
        def _(v):
            states = jnp.concatenate(
                [yrecv[0, c, v], yrecv[1, c, v], xrecv[0, v], xrecv[1, v], zeros], axis=0
            )
            high, low = split(states)
            change = product(cor[c], jnp.concatenate([high, low], axis=1))
            twice[v, rows] += change[:rows_c]
            fx[v, rows] += change[rows_c : 2 * rows_c]
            fy[v, rows] += change[2 * rows_c :]

        @pl.loop(0, rows_c // 16)
        def _(tile):
            at = pl.ds(pl.multiple_of(c * rows_c + tile * 16, 16), 16)
            density = rho[at]
            speed = [vel[d, at] for d in range(3)]
            square = 0.5 * (speed[0] * speed[0] + speed[1] * speed[1] + speed[2] * speed[2])
            enthalpy = (1.0 + 1.0 / GAMMA_LESS) * pre[at] / density + square
            first = [[f[v, at] for v in range(5)] for f in (fx, fy, fz)]
            heads = [
                g[1] * speed[0] + g[2] * speed[1] + g[3] * speed[2] + enthalpy * g[4] for g in first
            ]
            push = sum(g[1 + d] + speed[d] * g[4] for d, g in enumerate(first)) * GAMMA_LESS

            def carried(v):
                return speed[0] * first[0][v] + speed[1] * first[1][v] + speed[2] * first[2][v]

            conv = [
                square * push - (speed[0] * heads[0] + speed[1] * heads[1] + speed[2] * heads[2])
            ]
            for d in range(3):
                conv.append(carried(1 + d) + (first[d][0] + heads[d]) - speed[d] * push)
            conv.append(carried(4) + push)
            for v in range(5):
                out[v, at] = twice[v, at] - 2.0 * conv[v]

        write = pltpu.make_async_copy(out.at[:, rows], out_hbm.at[:, rows], out_sem.at[c])
        write.start()
        writes.append(write)

    for slot in range(2):
        for c in range(chunks):

            @pl.when(has[2 + slot])
            def _(slot=slot, c=c):
                y_copy(slot, c).wait_send()

        @pl.when(has[slot])
        def _(slot=slot):
            x_copy(slot).wait_send()

    for v in range(variables):
        z_copy(v).wait_send()
    for write in writes:
        write.wait()


def on_device(counts, adjoint, base_density, base_velocity, base_pressure):
    variables, nx, ny, nz = adjoint.shape
    cx = 8
    chunks = nx // cx
    rows = nx * ny
    local, state_y, state_x, correct, span = tables(nx, ny, nz, cx)
    field = (variables, rows, nz)
    y_shape = (2, chunks, variables, RANK * cx, nz)
    x_shape = (2, variables, RANK * ny, nz)
    dma = pltpu.SemaphoreType.DMA
    twice = pl.pallas_call(
        functools.partial(kernel, cx, counts),
        out_shape=jax.ShapeDtypeStruct(field, F32),
        in_specs=[pl.BlockSpec(memory_space=pl.ANY)] * 9,
        out_specs=pl.BlockSpec(memory_space=pl.ANY),
        scratch_shapes=[
            pltpu.VMEM(field, F32),
            pltpu.VMEM((rows, nz), F32),
            pltpu.VMEM((3, rows, nz), F32),
            pltpu.VMEM((rows, nz), F32),
            pltpu.VMEM(local.shape, BF16),
            pltpu.VMEM(state_y.shape, BF16),
            pltpu.VMEM(state_x.shape, BF16),
            pltpu.VMEM(correct.shape, BF16),
            pltpu.VMEM(span.shape, BF16),
            pltpu.VMEM((variables, rows, 2 * nz), BF16),
            pltpu.VMEM(field, F32),
            pltpu.VMEM(y_shape, F32),
            pltpu.VMEM(y_shape, F32),
            pltpu.VMEM(x_shape, F32),
            pltpu.VMEM(x_shape, F32),
            pltpu.VMEM(field, F32),
            pltpu.VMEM(field, F32),
            pltpu.VMEM(field, F32),
            pltpu.VMEM(field, F32),
            pltpu.VMEM(field, F32),
            dma((9,)),
            dma((chunks,)),
            dma((2, chunks)),
            dma((2, chunks)),
            dma((2,)),
            dma((2,)),
            dma((variables,)),
            dma((variables,)),
        ],
        compiler_params=pltpu.CompilerParams(
            collective_id=0, has_side_effects=True, vmem_limit_bytes=40 << 20
        ),
        name="adjoint_step",
    )(
        adjoint.reshape(field),
        base_density.reshape(rows, nz),
        base_velocity.reshape(3, rows, nz),
        base_pressure.reshape(rows, nz),
        local, state_y, state_x, correct, span,
    ).reshape(adjoint.shape)
    return 0.5 * twice, adjoint + 0.25 * twice


def solution(mesh):
    placed = (
        P(None, "gx", "gy", "gz"),
        P("gx", "gy", "gz"),
        P(None, "gx", "gy", "gz"),
        P("gx", "gy", "gz"),
    )
    return jax.shard_map(
        functools.partial(on_device, (mesh.shape["gx"], mesh.shape["gy"])),
        mesh=mesh,
        in_specs=placed,
        out_specs=(P(None, "gx", "gy", "gz"), P(None, "gx", "gy", "gz")),
        check_vma=False,
    )
```

```python
import functools

import jax
import jax.numpy as jnp
import numpy as np
from jax import lax
from jax.experimental import pallas as pl
from jax.experimental.pallas import tpu as pltpu
from jax.sharding import PartitionSpec as P

GAMMA_LESS = 0.4
RATIO = 1.0 / 3.0
COEF_NEAR = 7.0 / 9.0
COEF_FAR = 1.0 / 36.0
RANK = 4
F32 = jnp.float32
BF16 = jnp.bfloat16


def derivative(total, periodic):
    eye = np.eye(total)
    if periodic:
        up1, lo1, up2, lo2 = (np.roll(eye, s, axis=1) for s in (1, -1, 2, -2))
    else:
        up1, lo1, up2, lo2 = (np.eye(total, k=s) for s in (1, -1, 2, -2))
    banded = eye + RATIO * (up1 + lo1)
    stencil = COEF_NEAR * (up1 - lo1) + COEF_FAR * (up2 - lo2)
    return -stencil @ np.linalg.inv(banded)


def stacked(matrix, rows, cols):
    return np.vstack([(matrix @ matrix)[rows, cols], -2.0 * matrix[rows, cols]])


def line_factors(block):
    long = derivative(9 * block, False)
    near = derivative(4 * block, False)
    own = slice(4 * block, 5 * block)
    local = stacked(long, own, own)
    sides = []
    for beside, edge in (
        (slice(3 * block, 4 * block), slice(0, block)),
        (slice(5 * block, 6 * block), slice(3 * block, 4 * block)),
    ):
        basis, size, functional = np.linalg.svd(stacked(long, own, beside))
        basis = basis[:, :RANK]
        sides.append(
            (basis, size[:RANK, None] * functional[:RANK], basis.T @ (stacked(near, edge, edge) - local))
        )
    return local, sides


def four(matrix):
    high = matrix.astype(np.float32).astype(BF16)
    low = (matrix - high.astype(np.float64)).astype(np.float32).astype(BF16)
    return np.concatenate([high, high, low, low], axis=1)


def direction(block, lines):
    local, sides = line_factors(block)
    eye = np.eye(lines)
    state = np.stack(
        [
            np.stack([four(np.kron(eye, m)) for m in pair])
            for pair in ((sides[1][1], sides[0][2]), (sides[0][1], sides[1][2]))
        ]
    )
    whole = four(np.vstack([np.kron(eye, local[:block]), np.kron(eye, local[block:])]))
    change = four(
        np.vstack(
            [np.hstack([np.kron(eye, s[0][part]) for s in sides]) for part in (slice(0, block), slice(block, None))]
        )
    )
    return state, whole, change


@functools.lru_cache(maxsize=None)
def tables(nx, ny, nz):
    span = derivative(2 * nz, True)
    both = np.hstack([(span @ span)[:nz].T, -2.0 * span[:nz].T])
    high = both.astype(np.float32).astype(BF16)
    low = (both - high.astype(np.float64)).astype(np.float32).astype(BF16)
    return (*direction(ny, 4), *direction(nx, 2), np.stack([high, low]))


def split(value):
    high = value.astype(BF16)
    return high, (value - high.astype(F32)).astype(BF16)


def column(high, low):
    return jnp.concatenate([high, low, high, low], axis=0)


def dot(a, b):
    return jnp.dot(a, b, preferred_element_type=F32)


def pull(first, d, speed, square, enthalpy):
    head = first[1] * speed[0] + first[2] * speed[1] + first[3] * speed[2] + enthalpy * first[4]
    push = GAMMA_LESS * (first[1 + d] + speed[d] * first[4])
    result = [square * push - speed[d] * head]
    for i in range(3):
        term = speed[d] * first[1 + i] - speed[i] * push
        result.append(term + (first[0] + head) if i == d else term)
    result.append(speed[d] * first[4] + push)
    return result


def kernel(
    counts,
    adj_hbm, rho_hbm, vel_hbm, pre_hbm, sty_hbm, loy_hbm, chy_hbm, stx_hbm, lox_hbm, chx_hbm, spn_hbm,
    out_hbm,
    adj, rho, vel, pre, sty, loy, chy, stx, lox, chx, spn,
    highs, lows, other, ysend, yrecv, xsend, xrecv, twice, fy, tx, fx, squares, heats, out,
    adj_sem, in_sem, out_sem, ys_sem, yr_sem, xs_sem, xr_sem, zs_sem, zr_sem,
):
    gx, gy, gz = (lax.axis_index(n) for n in ("gx", "gy", "gz"))
    n_gx, n_gy = counts
    variables, rows_all, nz = adj.shape
    chunks = ysend.shape[1]
    rows_c = rows_all // chunks
    half = rows_c // 2
    ny = 16
    nx = rows_all // ny

    pieces = [
        pltpu.make_async_copy(
            adj_hbm.at[:, pl.ds(c * rows_c, rows_c)], adj.at[:, pl.ds(c * rows_c, rows_c)], adj_sem.at[c]
        )
        for c in range(chunks)
    ]
    loads = [
        pltpu.make_async_copy(src, dst, in_sem.at[k])
        for k, (src, dst) in enumerate(
            ((sty_hbm, sty), (loy_hbm, loy), (stx_hbm, stx), (lox_hbm, lox), (spn_hbm, spn),
             (rho_hbm, rho), (vel_hbm, vel), (pre_hbm, pre), (chx_hbm, chx), (chy_hbm, chy))
        )
    ]
    for load in pieces[:1] + loads[:2] + pieces[1:] + loads[2:]:
        load.start()

    has = (gx > 0, gx < n_gx - 1, gy > 0, gy < n_gy - 1)
    edge = tuple(jnp.where(there, 0, 1) for there in has)
    to = ({"gx": gx - 1}, {"gx": gx + 1}, {"gy": gy - 1}, {"gy": gy + 1})
    partner = {"gz": 1 - gz}
    barrier = pltpu.get_barrier_semaphore()
    for there, where in zip(has, to):

        @pl.when(there)
        def _(where=where):
            pl.semaphore_signal(barrier, inc=1, device_id=where, device_id_type=pl.DeviceIdType.MESH)

    pl.semaphore_signal(barrier, inc=1, device_id=partner, device_id_type=pl.DeviceIdType.MESH)
    neighbours = sum(jnp.where(there, 1, 0) for there in has) + 1

    def remote(src, dst, send, recv, where):
        return pltpu.make_async_remote_copy(
            src_ref=src, dst_ref=dst, send_sem=send, recv_sem=recv,
            device_id=where, device_id_type=pl.DeviceIdType.MESH,
        )

    def y_copy(slot, c):
        return remote(
            ysend.at[slot, c], yrecv.at[1 - slot, c], ys_sem.at[slot, c], yr_sem.at[1 - slot, c], to[2 + slot]
        )

    def x_copy(slot, v):
        return remote(
            xsend.at[slot, v], xrecv.at[1 - slot, v], xs_sem.at[slot, v], xr_sem.at[1 - slot, v], to[slot]
        )

    def z_copy(v):
        return remote(adj_hbm.at[v], other.at[v], zs_sem.at[v], zr_sem.at[v], partner)

    def y_part(c):
        rows = pl.ds(c * rows_c, rows_c)
        left = jnp.concatenate([sty[0, edge[2]], sty[1, edge[3]], loy[...]], axis=0)
        k = sty.shape[2]
        for v in range(variables):
            high, low = split(adj[v, rows])
            highs[v, rows] = high
            lows[v, rows] = low
            right = jnp.concatenate([column(high[:half], low[:half]), column(high[half:], low[half:])], axis=1)
            full = dot(left, right)
            for b in range(2):
                lanes = slice(b * nz, (b + 1) * nz)
                to_rows = pl.ds(c * rows_c + b * half, half)
                ysend[0, c, v, b] = full[:k, lanes]
                ysend[1, c, v, b] = full[k : 2 * k, lanes]
                twice[v, to_rows] = full[2 * k : 2 * k + half, lanes]
                fy[v, to_rows] = full[2 * k + half :, lanes]
        if c == 0:
            pl.semaphore_wait(barrier, neighbours)
        for slot in range(2):

            @pl.when(has[2 + slot])
            def _(slot=slot):
                y_copy(slot, c).start()

            @pl.when(jnp.logical_not(has[2 + slot]))
            def _(slot=slot):
                yrecv[slot, c] = ysend[slot, c]

    pieces[0].wait()
    loads[0].wait()
    loads[1].wait()
    y_part(0)
    for v in range(variables):
        z_copy(v).start()
    for c in range(1, chunks):
        pieces[c].wait()
    loads[2].wait()
    loads[3].wait()

    @pl.loop(0, variables)
    def _(v):
        left = jnp.concatenate([stx[0, edge[0]], stx[1, edge[1]], lox[...]], axis=0)
        k = stx.shape[2]
        for q in range(ny // 4):
            columns = []
            for b in range(2):
                lines = [adj[v, pl.ds(4 * q + 2 * b + j, nx, stride=ny)] for j in range(2)]
                columns.append(column(*split(jnp.concatenate(lines, axis=0))))
            full = dot(left, jnp.concatenate(columns, axis=1))
            for b in range(2):
                lanes = slice(b * nz, (b + 1) * nz)
                to_rows = pl.ds((4 * q + 2 * b) * nx, 2 * nx)
                xsend[0, v, 2 * q + b] = full[:k, lanes]
                xsend[1, v, 2 * q + b] = full[k : 2 * k, lanes]
                tx[v, to_rows] = full[2 * k : 2 * k + 2 * nx, lanes]
                fx[v, to_rows] = full[2 * k + 2 * nx :, lanes]
        for slot in range(2):

            @pl.when(has[slot])
            def _(slot=slot):
                x_copy(slot, v).start()

            @pl.when(jnp.logical_not(has[slot]))
            def _(slot=slot):
                xrecv[slot, v] = xsend[slot, v]

    for c in range(1, chunks):
        y_part(c)

    for load in loads[4:]:
        load.wait()
    for v in range(variables):
        z_copy(v).wait_recv()

    @pl.loop(0, variables)
    def _(v):
        high, low = split(other[v])
        high = jnp.concatenate([highs[v], high], axis=1)
        low = jnp.concatenate([lows[v], low], axis=1)
        full = dot(high, spn[0]) + dot(low, spn[0]) + dot(high, spn[1])
        twice[v] += full[:, :nz]
        other[v] = full[:, nz:]

    tile = 2 * ny

    @pl.loop(0, rows_all // tile)
    def _(t):
        at = pl.ds(pl.multiple_of(t * tile, tile), tile)
        speed = [vel[d, at] for d in range(3)]
        square = 0.5 * (speed[0] * speed[0] + speed[1] * speed[1] + speed[2] * speed[2])
        heat = (1.0 + 1.0 / GAMMA_LESS) * pre[at] / rho[at] + square
        squares[at] = square
        heats[at] = heat
        gained = pull([other[v, at] for v in range(5)], 2, speed, square, heat)
        for v in range(5):
            twice[v, at] += gained[v]

    @pl.loop(0, variables)
    def _(v):
        for slot in range(2):

            @pl.when(has[slot])
            def _(slot=slot):
                x_copy(1 - slot, v).wait_recv()

        for q in range(ny // 4):
            columns = [
                column(*split(jnp.concatenate([xrecv[slot, v, 2 * q + b] for slot in range(2)], axis=0)))
                for b in range(2)
            ]
            full = dot(chx[...], jnp.concatenate(columns, axis=1))
            for b in range(2):
                lanes = slice(b * nz, (b + 1) * nz)
                to_rows = pl.ds((4 * q + 2 * b) * nx, 2 * nx)
                tx[v, to_rows] += full[: 2 * nx, lanes]
                fx[v, to_rows] += full[2 * nx :, lanes]

    writes = []
    for c in range(chunks):
        rows = pl.ds(c * rows_c, rows_c)
        for slot in range(2):

            @pl.when(has[2 + slot])
            def _(slot=slot):
                y_copy(1 - slot, c).wait_recv()

        for v in range(variables):
            columns = [
                column(*split(jnp.concatenate([yrecv[slot, c, v, b] for slot in range(2)], axis=0)))
                for b in range(2)
            ]
            full = dot(chy[...], jnp.concatenate(columns, axis=1))
            for b in range(2):
                lanes = slice(b * nz, (b + 1) * nz)
                to_rows = pl.ds(c * rows_c + b * half, half)
                twice[v, to_rows] += full[:half, lanes]
                fy[v, to_rows] += full[half:, lanes]

        @pl.loop(0, rows_c // tile)
        def _(t):
            at = pl.ds(pl.multiple_of(c * rows_c + t * tile, tile), tile)
            first_line = c * (rows_c // ny) + t * (tile // ny)

            def turned(ref, v):
                return jnp.concatenate(
                    [ref[v, pl.ds(first_line + j, ny, stride=nx)] for j in range(tile // ny)], axis=0
                )

            speed = [vel[d, at] for d in range(3)]
            square, heat = squares[at], heats[at]
            by_x = pull([turned(fx, v) for v in range(5)], 0, speed, square, heat)
            by_y = pull([fy[v, at] for v in range(5)], 1, speed, square, heat)
            for v in range(5):
                out[v, at] = (twice[v, at] + turned(tx, v)) + (by_x[v] + by_y[v])

        write = pltpu.make_async_copy(out.at[:, rows], out_hbm.at[:, rows], out_sem.at[c])
        write.start()
        writes.append(write)

    for slot in range(2):
        for c in range(chunks):

            @pl.when(has[2 + slot])
            def _(slot=slot, c=c):
                y_copy(slot, c).wait_send()

        for v in range(variables):

            @pl.when(has[slot])
            def _(slot=slot, v=v):
                x_copy(slot, v).wait_send()

    for v in range(variables):
        z_copy(v).wait_send()
    for write in writes:
        write.wait()


def finish(twice_hbm, adj_hbm, tendency_hbm, updated_hbm, twice, adj, tendency, updated, in_sem, out_sem):
    variables = twice.shape[0]
    loads = [
        [
            pltpu.make_async_copy(twice_hbm.at[v], twice.at[v], in_sem.at[0, v]),
            pltpu.make_async_copy(adj_hbm.at[v], adj.at[v], in_sem.at[1, v]),
        ]
        for v in range(variables)
    ]
    for pair in loads:
        for load in pair:
            load.start()
    writes = []
    for v in range(variables):
        for load in loads[v]:
            load.wait()
        tendency[v] = 0.5 * twice[v]
        updated[v] = adj[v] + 0.25 * twice[v]
        for k, (src, dst) in enumerate(((tendency, tendency_hbm), (updated, updated_hbm))):
            write = pltpu.make_async_copy(src.at[v], dst.at[v], out_sem.at[k, v])
            write.start()
            writes.append(write)
    for write in writes:
        write.wait()


def on_device(counts, adjoint, base_density, base_velocity, base_pressure):
    variables, nx, ny, nz = adjoint.shape
    chunks = 3
    rows = nx * ny
    operators = tables(nx, ny, nz)
    field = (variables, rows, nz)
    y_shape = (2, chunks, variables, 2, 4 * RANK, nz)
    x_shape = (2, variables, ny // 2, 2 * RANK, nz)
    dma = pltpu.SemaphoreType.DMA
    hbm = pl.BlockSpec(memory_space=pl.ANY)
    whole = pltpu.VMEM(field, F32)
    whole_low = pltpu.VMEM(field, BF16)
    cells = pltpu.VMEM((rows, nz), F32)
    flat = adjoint.reshape(field)
    twice = pl.pallas_call(
        functools.partial(kernel, counts),
        out_shape=jax.ShapeDtypeStruct(field, F32),
        in_specs=[hbm] * 11,
        out_specs=hbm,
        scratch_shapes=[
            whole,
            cells,
            pltpu.VMEM((3, rows, nz), F32),
            cells,
            *[pltpu.VMEM(m.shape, BF16) for m in operators],
            whole_low,
            whole_low,
            whole,
            pltpu.VMEM(y_shape, F32),
            pltpu.VMEM(y_shape, F32),
            pltpu.VMEM(x_shape, F32),
            pltpu.VMEM(x_shape, F32),
            whole,
            whole,
            whole,
            whole,
            cells,
            cells,
            whole,
            dma((chunks,)),
            dma((10,)),
            dma((chunks,)),
            dma((2, chunks)),
            dma((2, chunks)),
            dma((2, variables)),
            dma((2, variables)),
            dma((variables,)),
            dma((variables,)),
        ],
        compiler_params=pltpu.CompilerParams(
            collective_id=0, has_side_effects=True, vmem_limit_bytes=62 << 20
        ),
        name="adjoint_step",
    )(
        flat,
        base_density.reshape(rows, nz),
        base_velocity.reshape(3, rows, nz),
        base_pressure.reshape(rows, nz),
        *operators,
    )
    tendency, updated = pl.pallas_call(
        finish,
        out_shape=[jax.ShapeDtypeStruct(field, F32)] * 2,
        in_specs=[hbm] * 2,
        out_specs=[hbm] * 2,
        scratch_shapes=[whole] * 4 + [dma((2, variables))] * 2,
        compiler_params=pltpu.CompilerParams(vmem_limit_bytes=62 << 20),
        name="finish",
    )(twice, flat)
    return tendency.reshape(adjoint.shape), updated.reshape(adjoint.shape)


def solution(mesh):
    placed = (
        P(None, "gx", "gy", "gz"),
        P("gx", "gy", "gz"),
        P(None, "gx", "gy", "gz"),
        P("gx", "gy", "gz"),
    )
    return jax.shard_map(
        functools.partial(on_device, (mesh.shape["gx"], mesh.shape["gy"])),
        mesh=mesh,
        in_specs=placed,
        out_specs=(P(None, "gx", "gy", "gz"), P(None, "gx", "gy", "gz")),
        check_vma=False,
    )
```

```python
import functools

import jax
import jax.numpy as jnp
import numpy as np
from jax import lax
from jax.experimental import pallas as pl
from jax.experimental.pallas import tpu as pltpu
from jax.sharding import PartitionSpec as P

GAMMA_LESS = 0.4
RATIO = 1.0 / 3.0
COEF_NEAR = 7.0 / 9.0
COEF_FAR = 1.0 / 36.0
RANK = 4
F32 = jnp.float32
BF16 = jnp.bfloat16


def derivative(total, periodic):
    eye = np.eye(total)
    if periodic:
        up1, lo1, up2, lo2 = (np.roll(eye, s, axis=1) for s in (1, -1, 2, -2))
    else:
        up1, lo1, up2, lo2 = (np.eye(total, k=s) for s in (1, -1, 2, -2))
    banded = eye + RATIO * (up1 + lo1)
    stencil = COEF_NEAR * (up1 - lo1) + COEF_FAR * (up2 - lo2)
    return -stencil @ np.linalg.inv(banded)


def stacked(matrix, rows, cols):
    return np.vstack([(matrix @ matrix)[rows, cols], -2.0 * matrix[rows, cols]])


def line_factors(block):
    long = derivative(9 * block, False)
    near = derivative(4 * block, False)
    own = slice(4 * block, 5 * block)
    local = stacked(long, own, own)
    sides = []
    for beside, edge in (
        (slice(3 * block, 4 * block), slice(0, block)),
        (slice(5 * block, 6 * block), slice(3 * block, 4 * block)),
    ):
        basis, size, functional = np.linalg.svd(stacked(long, own, beside))
        basis = basis[:, :RANK]
        sides.append(
            (basis, size[:RANK, None] * functional[:RANK], basis.T @ (stacked(near, edge, edge) - local))
        )
    return local, sides


def four(matrix):
    high = matrix.astype(np.float32).astype(BF16)
    low = (matrix - high.astype(np.float64)).astype(np.float32).astype(BF16)
    return np.concatenate([high, high, low, low], axis=1)


def direction(block, lines):
    local, sides = line_factors(block)
    eye = np.eye(lines)
    state = np.stack(
        [
            np.stack([four(np.kron(eye, m)) for m in pair])
            for pair in ((sides[1][1], sides[0][2]), (sides[0][1], sides[1][2]))
        ]
    )
    whole = four(np.vstack([np.kron(eye, local[:block]), np.kron(eye, local[block:])]))
    change = four(
        np.vstack(
            [np.hstack([np.kron(eye, s[0][part]) for s in sides]) for part in (slice(0, block), slice(block, None))]
        )
    )
    return state, whole, change


@functools.lru_cache(maxsize=None)
def tables(nx, ny, nz):
    span = derivative(2 * nz, True)
    both = np.hstack([(span @ span)[:nz].T, -2.0 * span[:nz].T])
    high = both.astype(np.float32).astype(BF16)
    low = (both - high.astype(np.float64)).astype(np.float32).astype(BF16)
    return (*direction(ny, 4), *direction(nx, 2), np.stack([high, low]))


def split(value):
    high = value.astype(BF16)
    return high, (value - high.astype(F32)).astype(BF16)


def column(high, low):
    return jnp.concatenate([high, low, high, low], axis=0)


def dot(a, b):
    return jnp.dot(a, b, preferred_element_type=F32)


def pull(first, d, speed, square, enthalpy):
    head = first[1] * speed[0] + first[2] * speed[1] + first[3] * speed[2] + enthalpy * first[4]
    push = GAMMA_LESS * (first[1 + d] + speed[d] * first[4])
    result = [square * push - speed[d] * head]
    for i in range(3):
        term = speed[d] * first[1 + i] - speed[i] * push
        result.append(term + (first[0] + head) if i == d else term)
    result.append(speed[d] * first[4] + push)
    return result


def kernel(
    counts,
    adj_hbm, rho_hbm, vel_hbm, pre_hbm, sty_hbm, loy_hbm, chy_hbm, stx_hbm, lox_hbm, chx_hbm, spn_hbm,
    tendency, updated,
    adj, rho, vel, pre, sty, loy, chy, stx, lox, chx, spn,
    highs, lows, other, ysend, yrecv, xsend, xrecv, twice, fy, tx, fx, squares, heats,
    adj_sem, in_sem, ys_sem, yr_sem, xs_sem, xr_sem, zs_sem, zr_sem,
):
    gx, gy, gz = (lax.axis_index(n) for n in ("gx", "gy", "gz"))
    n_gx, n_gy = counts
    variables, rows_all, nz = adj.shape
    chunks = ysend.shape[1]
    rows_c = rows_all // chunks
    half = rows_c // 2
    ny = 16
    nx = rows_all // ny

    pieces = [
        pltpu.make_async_copy(
            adj_hbm.at[:, pl.ds(c * rows_c, rows_c)], adj.at[:, pl.ds(c * rows_c, rows_c)], adj_sem.at[c]
        )
        for c in range(chunks)
    ]
    loads = [
        pltpu.make_async_copy(src, dst, in_sem.at[k])
        for k, (src, dst) in enumerate(
            ((sty_hbm, sty), (loy_hbm, loy), (stx_hbm, stx), (lox_hbm, lox), (spn_hbm, spn),
             (rho_hbm, rho), (vel_hbm, vel), (pre_hbm, pre), (chx_hbm, chx), (chy_hbm, chy))
        )
    ]
    for load in pieces[:1] + loads[:2] + pieces[1:] + loads[2:]:
        load.start()

    has = (gx > 0, gx < n_gx - 1, gy > 0, gy < n_gy - 1)
    edge = tuple(jnp.where(there, 0, 1) for there in has)
    to = ({"gx": gx - 1}, {"gx": gx + 1}, {"gy": gy - 1}, {"gy": gy + 1})
    partner = {"gz": 1 - gz}
    barrier = pltpu.get_barrier_semaphore()
    for there, where in zip(has, to):

        @pl.when(there)
        def _(where=where):
            pl.semaphore_signal(barrier, inc=1, device_id=where, device_id_type=pl.DeviceIdType.MESH)

    pl.semaphore_signal(barrier, inc=1, device_id=partner, device_id_type=pl.DeviceIdType.MESH)
    neighbours = sum(jnp.where(there, 1, 0) for there in has) + 1

    def remote(src, dst, send, recv, where):
        return pltpu.make_async_remote_copy(
            src_ref=src, dst_ref=dst, send_sem=send, recv_sem=recv,
            device_id=where, device_id_type=pl.DeviceIdType.MESH,
        )

    def y_copy(slot, c):
        return remote(
            ysend.at[slot, c], yrecv.at[1 - slot, c], ys_sem.at[slot, c], yr_sem.at[1 - slot, c], to[2 + slot]
        )

    def x_copy(slot, v):
        return remote(
            xsend.at[slot, v], xrecv.at[1 - slot, v], xs_sem.at[slot, v], xr_sem.at[1 - slot, v], to[slot]
        )

    def z_copy(v):
        return remote(adj_hbm.at[v], other.at[v], zs_sem.at[v], zr_sem.at[v], partner)

    def y_part(c):
        rows = pl.ds(c * rows_c, rows_c)
        left = jnp.concatenate([sty[0, edge[2]], sty[1, edge[3]], loy[...]], axis=0)
        k = sty.shape[2]
        for v in range(variables):
            high, low = split(adj[v, rows])
            highs[v, rows] = high
            lows[v, rows] = low
            right = jnp.concatenate([column(high[:half], low[:half]), column(high[half:], low[half:])], axis=1)
            full = dot(left, right)
            for b in range(2):
                lanes = slice(b * nz, (b + 1) * nz)
                to_rows = pl.ds(c * rows_c + b * half, half)
                ysend[0, c, v, b] = full[:k, lanes]
                ysend[1, c, v, b] = full[k : 2 * k, lanes]
                twice[v, to_rows] = full[2 * k : 2 * k + half, lanes]
                fy[v, to_rows] = full[2 * k + half :, lanes]
        if c == 0:
            pl.semaphore_wait(barrier, neighbours)
        for slot in range(2):

            @pl.when(has[2 + slot])
            def _(slot=slot):
                y_copy(slot, c).start()

            @pl.when(jnp.logical_not(has[2 + slot]))
            def _(slot=slot):
                yrecv[slot, c] = ysend[slot, c]

    pieces[0].wait()
    loads[0].wait()
    loads[1].wait()
    y_part(0)
    for v in range(variables):
        z_copy(v).start()
    for c in range(1, chunks):
        pieces[c].wait()
    loads[2].wait()
    loads[3].wait()

    @pl.loop(0, variables)
    def _(v):
        left = jnp.concatenate([stx[0, edge[0]], stx[1, edge[1]], lox[...]], axis=0)
        k = stx.shape[2]
        for q in range(ny // 4):
            columns = []
            for b in range(2):
                lines = [adj[v, pl.ds(4 * q + 2 * b + j, nx, stride=ny)] for j in range(2)]
                columns.append(column(*split(jnp.concatenate(lines, axis=0))))
            full = dot(left, jnp.concatenate(columns, axis=1))
            for b in range(2):
                lanes = slice(b * nz, (b + 1) * nz)
                to_rows = pl.ds((4 * q + 2 * b) * nx, 2 * nx)
                xsend[0, v, 2 * q + b] = full[:k, lanes]
                xsend[1, v, 2 * q + b] = full[k : 2 * k, lanes]
                tx[v, to_rows] = full[2 * k : 2 * k + 2 * nx, lanes]
                fx[v, to_rows] = full[2 * k + 2 * nx :, lanes]
        for slot in range(2):

            @pl.when(has[slot])
            def _(slot=slot):
                x_copy(slot, v).start()

            @pl.when(jnp.logical_not(has[slot]))
            def _(slot=slot):
                xrecv[slot, v] = xsend[slot, v]

    for c in range(1, chunks):
        y_part(c)

    for load in loads[4:]:
        load.wait()
    for v in range(variables):
        z_copy(v).wait_recv()

    @pl.loop(0, variables)
    def _(v):
        high, low = split(other[v])
        high = jnp.concatenate([highs[v], high], axis=1)
        low = jnp.concatenate([lows[v], low], axis=1)
        full = dot(high, spn[0]) + dot(low, spn[0]) + dot(high, spn[1])
        twice[v] += full[:, :nz]
        other[v] = full[:, nz:]

    tile = 2 * ny

    @pl.loop(0, rows_all // tile)
    def _(t):
        at = pl.ds(pl.multiple_of(t * tile, tile), tile)
        speed = [vel[d, at] for d in range(3)]
        square = 0.5 * (speed[0] * speed[0] + speed[1] * speed[1] + speed[2] * speed[2])
        heat = (1.0 + 1.0 / GAMMA_LESS) * pre[at] / rho[at] + square
        squares[at] = square
        heats[at] = heat
        gained = pull([other[v, at] for v in range(5)], 2, speed, square, heat)
        for v in range(5):
            twice[v, at] += gained[v]

    @pl.loop(0, variables)
    def _(v):
        for slot in range(2):

            @pl.when(has[slot])
            def _(slot=slot):
                x_copy(1 - slot, v).wait_recv()

        for q in range(ny // 4):
            columns = [
                column(*split(jnp.concatenate([xrecv[slot, v, 2 * q + b] for slot in range(2)], axis=0)))
                for b in range(2)
            ]
            full = dot(chx[...], jnp.concatenate(columns, axis=1))
            for b in range(2):
                lanes = slice(b * nz, (b + 1) * nz)
                to_rows = pl.ds((4 * q + 2 * b) * nx, 2 * nx)
                tx[v, to_rows] += full[: 2 * nx, lanes]
                fx[v, to_rows] += full[2 * nx :, lanes]

    for c in range(chunks):
        for slot in range(2):

            @pl.when(has[2 + slot])
            def _(slot=slot):
                y_copy(1 - slot, c).wait_recv()

        for v in range(variables):
            columns = [
                column(*split(jnp.concatenate([yrecv[slot, c, v, b] for slot in range(2)], axis=0)))
                for b in range(2)
            ]
            full = dot(chy[...], jnp.concatenate(columns, axis=1))
            for b in range(2):
                lanes = slice(b * nz, (b + 1) * nz)
                to_rows = pl.ds(c * rows_c + b * half, half)
                twice[v, to_rows] += full[:half, lanes]
                fy[v, to_rows] += full[half:, lanes]

        @pl.loop(0, rows_c // tile)
        def _(t):
            at = pl.ds(pl.multiple_of(c * rows_c + t * tile, tile), tile)
            first_line = c * (rows_c // ny) + t * (tile // ny)

            def turned(ref, v):
                return jnp.concatenate(
                    [ref[v, pl.ds(first_line + j, ny, stride=nx)] for j in range(tile // ny)], axis=0
                )

            speed = [vel[d, at] for d in range(3)]
            square, heat = squares[at], heats[at]
            by_x = pull([turned(fx, v) for v in range(5)], 0, speed, square, heat)
            by_y = pull([fy[v, at] for v in range(5)], 1, speed, square, heat)
            for v in range(5):
                total = (twice[v, at] + turned(tx, v)) + (by_x[v] + by_y[v])
                tendency[v, at] = 0.5 * total
                updated[v, at] = adj[v, at] + 0.25 * total

    for slot in range(2):
        for c in range(chunks):

            @pl.when(has[2 + slot])
            def _(slot=slot, c=c):
                y_copy(slot, c).wait_send()

        for v in range(variables):

            @pl.when(has[slot])
            def _(slot=slot, v=v):
                x_copy(slot, v).wait_send()

    for v in range(variables):
        z_copy(v).wait_send()


def finish(tendency, updated, tendency_hbm, updated_hbm, sem):
    writes = [
        pltpu.make_async_copy(src, dst, sem.at[k])
        for k, (src, dst) in enumerate(((tendency, tendency_hbm), (updated, updated_hbm)))
    ]
    for write in writes:
        write.start()
    for write in writes:
        write.wait()


def on_device(counts, adjoint, base_density, base_velocity, base_pressure):
    variables, nx, ny, nz = adjoint.shape
    chunks = 3
    rows = nx * ny
    operators = tables(nx, ny, nz)
    field = (variables, rows, nz)
    y_shape = (2, chunks, variables, 2, 4 * RANK, nz)
    x_shape = (2, variables, ny // 2, 2 * RANK, nz)
    dma = pltpu.SemaphoreType.DMA
    hbm = pl.BlockSpec(memory_space=pl.ANY)
    whole = pltpu.VMEM(field, F32)
    whole_low = pltpu.VMEM(field, BF16)
    cells = pltpu.VMEM((rows, nz), F32)
    tendency, updated = pl.pallas_call(
        functools.partial(kernel, counts),
        out_shape=[pltpu.VMEM(field, F32)] * 2,
        in_specs=[hbm] * 11,
        out_specs=[pl.BlockSpec(memory_space=pltpu.VMEM)] * 2,
        scratch_shapes=[
            whole,
            cells,
            pltpu.VMEM((3, rows, nz), F32),
            cells,
            *[pltpu.VMEM(m.shape, BF16) for m in operators],
            whole_low,
            whole_low,
            whole,
            pltpu.VMEM(y_shape, F32),
            pltpu.VMEM(y_shape, F32),
            pltpu.VMEM(x_shape, F32),
            pltpu.VMEM(x_shape, F32),
            whole,
            whole,
            whole,
            whole,
            cells,
            cells,
            dma((chunks,)),
            dma((10,)),
            dma((2, chunks)),
            dma((2, chunks)),
            dma((2, variables)),
            dma((2, variables)),
            dma((variables,)),
            dma((variables,)),
        ],
        compiler_params=pltpu.CompilerParams(
            collective_id=0, has_side_effects=True, vmem_limit_bytes=32 << 20
        ),
        name="adjoint_step",
    )(
        *[
            pltpu.with_memory_space_constraint(jnp.asarray(x), pltpu.HBM)
            for x in (
                adjoint.reshape(field),
                base_density.reshape(rows, nz),
                base_velocity.reshape(3, rows, nz),
                base_pressure.reshape(rows, nz),
                *operators,
            )
        ]
    )
    tendency, updated = pl.pallas_call(
        finish,
        out_shape=[jax.ShapeDtypeStruct(field, F32)] * 2,
        in_specs=[pl.BlockSpec(memory_space=pltpu.VMEM)] * 2,
        out_specs=[hbm] * 2,
        scratch_shapes=[dma((2,))],
        compiler_params=pltpu.CompilerParams(vmem_limit_bytes=16 << 20),
        name="finish",
    )(*[pltpu.with_memory_space_constraint(x, pltpu.VMEM) for x in (tendency, updated)])
    return tendency.reshape(adjoint.shape), updated.reshape(adjoint.shape)


def solution(mesh):
    placed = (
        P(None, "gx", "gy", "gz"),
        P("gx", "gy", "gz"),
        P(None, "gx", "gy", "gz"),
        P("gx", "gy", "gz"),
    )
    return jax.shard_map(
        functools.partial(on_device, (mesh.shape["gx"], mesh.shape["gy"])),
        mesh=mesh,
        in_specs=placed,
        out_specs=(P(None, "gx", "gy", "gz"), P(None, "gx", "gy", "gz")),
        check_vma=False,
    )
```

```python
import functools

import jax
import jax.numpy as jnp
import numpy as np
from jax import lax
from jax.experimental import pallas as pl
from jax.experimental.pallas import tpu as pltpu
from jax.sharding import PartitionSpec as P

GAMMA_LESS = 0.4
RATIO = 1.0 / 3.0
COEF_NEAR = 7.0 / 9.0
COEF_FAR = 1.0 / 36.0
RANK = 4
THIN = True
SENT = 24 if THIN else 32
EDGE = 16
F32 = jnp.float32
BF16 = jnp.bfloat16


def derivative(total, periodic):
    eye = np.eye(total)
    if periodic:
        up1, lo1, up2, lo2 = (np.roll(eye, s, axis=1) for s in (1, -1, 2, -2))
    else:
        up1, lo1, up2, lo2 = (np.eye(total, k=s) for s in (1, -1, 2, -2))
    banded = eye + RATIO * (up1 + lo1)
    stencil = COEF_NEAR * (up1 - lo1) + COEF_FAR * (up2 - lo2)
    return -stencil @ np.linalg.inv(banded)


def stacked(matrix, rows, cols):
    return np.vstack([(matrix @ matrix)[rows, cols], -2.0 * matrix[rows, cols]])


def line_factors(block, thin):
    long = derivative(9 * block, False)
    near = derivative(4 * block, False)
    own = slice(4 * block, 5 * block)
    local = stacked(long, own, own)
    sides = []
    for beside, edge in (
        (slice(3 * block, 4 * block), slice(0, block)),
        (slice(5 * block, 6 * block), slice(3 * block, 4 * block)),
    ):
        basis, size, functional = np.linalg.svd(stacked(long, own, beside))
        basis, size, functional = basis[:, :RANK], size[:RANK], functional[:RANK]
        end = (basis, basis.T @ (stacked(near, edge, edge) - local))
        if thin:
            flat = functional.sum(axis=1)
            unseen = np.eye(RANK)[-1] - flat * flat[-1] / (flat @ flat)
            left_out = unseen / size**2
            left_out /= unseen @ left_out
            kept = np.linalg.svd(left_out[None])[2][1:].T
            basis, mixed = np.linalg.qr((basis * size) @ (np.eye(RANK) - np.outer(left_out, unseen)) @ kept)
            sides.append(((basis, mixed @ kept.T @ functional), end))
        else:
            sides.append(((basis, size[:, None] * functional), end))
    return local, sides


def four(matrix):
    high = matrix.astype(np.float32).astype(BF16)
    low = (matrix - high.astype(np.float64)).astype(np.float32).astype(BF16)
    return np.concatenate([high, high, low, low], axis=1)


def direction(block, lines, thin):
    local, sides = line_factors(block, thin)
    eye = np.eye(lines)
    order = [(slice(0, 2), slice(2, 3), slice(2, 3) if thin else slice(3, 4)), (slice(0, 2), slice(2, 3), slice(3, 4))]
    state = np.stack(
        [
            np.stack(
                [
                    four(np.vstack([np.kron(eye, factors[1][part]) for part in order[end]]))
                    for end, factors in enumerate(pair)
                ]
            )
            for pair in ((sides[1][0], sides[0][1]), (sides[0][0], sides[1][1]))
        ]
    )
    whole = four(np.vstack([np.kron(eye, local[:block]), np.kron(eye, local[block:])]))

    def gained(ends):
        return np.vstack(
            [
                np.hstack(
                    [np.kron(eye, side[end][0][half, part]) for side, end in zip(sides, ends) for part in order[end]]
                )
                for half in (slice(0, block), slice(block, None))
            ]
        )

    change = np.stack([np.stack([four(gained((a, b))) for b in range(2)]) for a in range(2)])
    both = np.concatenate([np.broadcast_to(whole, change.shape[:2] + whole.shape), change], axis=-1)
    return state, whole, change, both


def span_table(nz):
    span = derivative(2 * nz, True)
    both = np.hstack([(span @ span)[:nz].T, -2.0 * span[:nz].T])
    high = both.astype(np.float32).astype(BF16)
    low = (both - high.astype(np.float64)).astype(np.float32).astype(BF16)
    first, last = [nz + k for k in range(EDGE)], [2 * nz - EDGE + k for k in range(EDGE)]
    rest = np.zeros((nz - 6 * EDGE, 2 * nz), BF16)
    second = np.concatenate(
        [low[:nz], high[first], high[last], high[first], low[last], low[first], rest, high[last]], axis=0
    )
    return np.stack([np.concatenate([high[:nz], high[:nz]], axis=0), second])


@functools.lru_cache(maxsize=None)
def tables(nx, ny, nz):
    state_y, local_y, change_y, _ = direction(ny, 4, THIN)
    state_x, _, _, both_x = direction(nx, 2, False)
    return state_y, local_y, change_y, state_x, both_x, span_table(nz)


def split(value):
    high = value.astype(BF16)
    return high, (value - high.astype(F32)).astype(BF16)


def column(high, low):
    return jnp.concatenate([high, low, high, low], axis=0)


def dot(a, b):
    return jnp.dot(a, b, preferred_element_type=F32)


def pull(first, d, speed, square, enthalpy):
    head = first[1] * speed[0] + first[2] * speed[1] + first[3] * speed[2] + enthalpy * first[4]
    push = GAMMA_LESS * (first[1 + d] + speed[d] * first[4])
    result = [square * push - speed[d] * head]
    for i in range(3):
        term = speed[d] * first[1 + i] - speed[i] * push
        result.append(term + (first[0] + head) if i == d else term)
    result.append(speed[d] * first[4] + push)
    return result


def pull_two(g, k, speed, square, enthalpy):
    head_g = g[1] * speed[0] + g[2] * speed[1] + g[3] * speed[2] + enthalpy * g[4]
    head_k = k[1] * speed[0] + k[2] * speed[1] + k[3] * speed[2] + enthalpy * k[4]
    energy = speed[0] * g[4] + speed[1] * k[4]
    push = GAMMA_LESS * ((g[1] + k[2]) + energy)
    return [
        square * push - (speed[0] * head_g + speed[1] * head_k),
        (speed[0] * (g[1] - push) + speed[1] * k[1]) + (g[0] + head_g),
        (speed[0] * g[2] + speed[1] * (k[2] - push)) + (k[0] + head_k),
        speed[0] * g[3] + speed[1] * k[3] - speed[2] * push,
        energy + push,
    ]


def kernel(
    counts,
    adj_hbm, rho_hbm, vel_hbm, pre_hbm, sty_hbm, loy_hbm, chy_hbm, stx_hbm, chx_hbm, spn_hbm,
    tendency, updated,
    adj, rho, vel, pre, sty, loy, chy, stx, chx, spn,
    highs, lows, turned, other, ysend, yrecv, xsend, xrecv, twice, fy, tx, fx, tz, squares, heats,
    adj_sem, in_sem, ys_sem, yr_sem, xs_sem, xr_sem, zs_sem, zr_sem,
):
    gx, gy, gz = (lax.axis_index(n) for n in ("gx", "gy", "gz"))
    n_gx, n_gy = counts
    variables, rows_all, nz = adj.shape
    chunks = ysend.shape[1]
    rows_c = rows_all // chunks
    half = rows_c // 2
    ny = 16
    nx = rows_all // ny

    pieces = [
        pltpu.make_async_copy(
            adj_hbm.at[:, pl.ds(c * rows_c, rows_c)], adj.at[:, pl.ds(c * rows_c, rows_c)], adj_sem.at[c]
        )
        for c in range(chunks)
    ]
    loads = [
        pltpu.make_async_copy(src, dst, in_sem.at[k])
        for k, (src, dst) in enumerate(
            ((sty_hbm, sty), (stx_hbm, stx), (loy_hbm, loy), (spn_hbm, spn),
             (rho_hbm, rho), (vel_hbm, vel), (pre_hbm, pre), (chx_hbm, chx), (chy_hbm, chy))
        )
    ]
    pieces[0].start()
    loads[0].start()

    has = (gx > 0, gx < n_gx - 1, gy > 0, gy < n_gy - 1)
    edge = tuple(jnp.where(there, 0, 1) for there in has)
    to = ({"gx": gx - 1}, {"gx": gx + 1}, {"gy": gy - 1}, {"gy": gy + 1})
    partner = {"gz": 1 - gz}
    lane = lax.broadcasted_iota(jnp.int32, (rows_all, nz), 1)
    upper = lax.broadcasted_iota(jnp.int32, (8, nz), 0) < 4
    own_rest = tuple(jnp.logical_not(there) if THIN else True for there in has)
    barrier = pltpu.get_barrier_semaphore()
    for there, where in zip(has, to):

        @pl.when(there)
        def _(where=where):
            pl.semaphore_signal(barrier, inc=1, device_id=where, device_id_type=pl.DeviceIdType.MESH)

    pl.semaphore_signal(barrier, inc=1, device_id=partner, device_id_type=pl.DeviceIdType.MESH)
    for load in pieces[1:] + loads[1:]:
        load.start()
    neighbours = sum(jnp.where(there, 1, 0) for there in has) + 1

    def remote(src, dst, send, recv, where):
        return pltpu.make_async_remote_copy(
            src_ref=src, dst_ref=dst, send_sem=send, recv_sem=recv,
            device_id=where, device_id_type=pl.DeviceIdType.MESH,
        )

    def y_copy(slot, c):
        return remote(
            ysend.at[slot, c, :, pl.ds(0, SENT)], yrecv.at[1 - slot, c, :, pl.ds(0, SENT)], ys_sem.at[slot, c], yr_sem.at[1 - slot, c], to[2 + slot]
        )

    def x_copy(slot, v):
        return remote(
            xsend.at[slot, v], xrecv.at[1 - slot, v], xs_sem.at[slot, v], xr_sem.at[1 - slot, v], to[slot]
        )

    def z_copy(v):
        return remote(adj_hbm.at[v], other.at[v], zs_sem.at[v], zr_sem.at[v], partner)

    def y_part(c):
        rows = pl.ds(c * rows_c, rows_c)
        left = jnp.concatenate([sty[0, edge[2]], sty[1, edge[3]]], axis=0)
        k = sty.shape[2]
        for v in range(variables):
            high, low = split(adj[v, rows])
            highs[v, rows] = high
            lows[v, rows] = low
            right = jnp.concatenate([column(high[:half], low[:half]), column(high[half:], low[half:])], axis=1)
            full = dot(left, right)
            for slot in range(2):
                pair, rest = full[slot * k : slot * k + 8], full[slot * k + 8 : (slot + 1) * k]
                ysend[slot, c, v, :8] = pair[:, :nz]
                ysend[slot, c, v, 8:16] = pair[:, nz:]
                ysend[slot, c, v, 16:24] = jnp.where(upper | own_rest[2 + slot], rest[:, :nz], rest[:, nz:])
                ysend[slot, c, v, 24:] = rest[:, nz:]
        if c == 0:
            pl.semaphore_wait(barrier, neighbours)
        for slot in range(2):

            @pl.when(has[2 + slot])
            def _(slot=slot):
                y_copy(slot, c).start()

            @pl.when(jnp.logical_not(has[2 + slot]))
            def _(slot=slot):
                yrecv[slot, c] = ysend[slot, c]

    pieces[0].wait()
    loads[0].wait()
    y_part(0)
    for v in range(variables):
        z_copy(v).start()
    for c in range(1, chunks):
        pieces[c].wait()
    loads[1].wait()
    loads[2].wait()

    @pl.loop(0, variables)
    def _(v):
        left = jnp.concatenate([stx[0, edge[0]], stx[1, edge[1]]], axis=0)
        k = stx.shape[2]
        for q in range(ny // 4):
            halves = []
            for b in range(2):
                lines = [adj[v, pl.ds(4 * q + 2 * b + j, nx, stride=ny)] for j in range(2)]
                halves.append(jnp.concatenate(split(jnp.concatenate(lines, axis=0)), axis=0))
            lined = jnp.concatenate(halves, axis=1)
            turned[v, q] = lined
            full = dot(left, jnp.concatenate([lined, lined], axis=0))
            for b in range(2):
                lanes = slice(b * nz, (b + 1) * nz)
                xsend[0, v, 2 * q + b] = full[:k, lanes]
                xsend[1, v, 2 * q + b] = full[k : 2 * k, lanes]
        for slot in range(2):

            @pl.when(has[slot])
            def _(slot=slot):
                x_copy(slot, v).start()

            @pl.when(jnp.logical_not(has[slot]))
            def _(slot=slot):
                xrecv[slot, v] = xsend[slot, v]

    for c in range(1, chunks):
        y_part(c)

    for load in loads[3:]:
        load.wait()
    for c in range(chunks):
        rows = pl.ds(c * rows_c, rows_c)
        for v in range(variables):
            high, low = highs[v, rows], lows[v, rows]
            full = dot(
                loy[...],
                jnp.concatenate([column(high[:half], low[:half]), column(high[half:], low[half:])], axis=1),
            )
            for b in range(2):
                lanes = slice(b * nz, (b + 1) * nz)
                to_rows = pl.ds(c * rows_c + b * half, half)
                twice[v, to_rows] = full[:half, lanes]
                fy[v, to_rows] = full[half:, lanes]

    for v in range(variables):
        z_copy(v).wait_recv()

    for v in range(variables):
        theirs = other[v]
        at_low = pltpu.roll(theirs, 2 * EDGE, 1)
        at_low = at_low - at_low.astype(BF16).astype(F32)
        ends = jnp.where((lane >= EDGE) & (lane < 3 * EDGE), at_low, theirs)
        ends = jnp.where((lane >= 3 * EDGE) & (lane < 5 * EDGE), pltpu.roll(theirs, 4 * EDGE, 1), ends).astype(BF16)
        high = highs[v]
        full = dot(jnp.concatenate([high, lows[v]], axis=1), spn[0]) + dot(
            jnp.concatenate([high, ends], axis=1), spn[1]
        )
        tz[v] = full[:, :nz]
        other[v] = full[:, nz:]

    tile = 2 * ny

    @pl.loop(0, rows_all // tile)
    def _(t):
        at = pl.ds(pl.multiple_of(t * tile, tile), tile)
        speed = [vel[d, at] for d in range(3)]
        square = 0.5 * (speed[0] * speed[0] + speed[1] * speed[1] + speed[2] * speed[2])
        heat = (1.0 + 1.0 / GAMMA_LESS) * pre[at] / rho[at] + square
        squares[at] = square
        heats[at] = heat
        gained = pull([other[v, at] for v in range(5)], 2, speed, square, heat)
        for v in range(5):
            tz[v, at] += gained[v]

    def y_fix(c):
        rows = pl.ds(c * rows_c, rows_c)
        for slot in range(2):

            @pl.when(has[2 + slot])
            def _(slot=slot):
                y_copy(1 - slot, c).wait_recv()

        for v in range(variables):
            parts = ([], [])
            for slot in range(2):
                rest, last = yrecv[slot, c, v, 16:24], yrecv[slot, c, v, 24:]
                parts[0].extend([yrecv[slot, c, v, :8], jnp.where(upper | own_rest[2 + slot], rest, 0.0)])
                parts[1].extend(
                    [yrecv[slot, c, v, 8:16], jnp.where(own_rest[2 + slot], last, jnp.where(upper, 0.0, rest))]
                )
            columns = [column(*split(jnp.concatenate(part, axis=0))) for part in parts]
            full = dot(chy[edge[2], edge[3]], jnp.concatenate(columns, axis=1))
            for b in range(2):
                lanes = slice(b * nz, (b + 1) * nz)
                to_rows = pl.ds(c * rows_c + b * half, half)
                twice[v, to_rows] += full[:half, lanes]
                fy[v, to_rows] += full[half:, lanes]

    def combine(c):
        @pl.loop(0, rows_c // tile)
        def _(t):
            at = pl.ds(pl.multiple_of(c * rows_c + t * tile, tile), tile)
            first_line = c * (rows_c // ny) + t * (tile // ny)

            def natural(ref, v):
                return jnp.concatenate(
                    [ref[v, pl.ds(first_line + j, ny, stride=nx)] for j in range(tile // ny)], axis=0
                )

            speed = [vel[d, at] for d in range(3)]
            square, heat = squares[at], heats[at]
            gain = pull_two(
                [natural(fx, v) for v in range(5)], [fy[v, at] for v in range(5)], speed, square, heat
            )
            for v in range(5):
                total = (twice[v, at] + natural(tx, v)) + (tz[v, at] + gain[v])
                tendency[v, at] = 0.5 * total
                updated[v, at] = adj[v, at] + 0.25 * total

    y_fix(0)

    @pl.loop(0, variables)
    def _(v):
        for slot in range(2):

            @pl.when(has[slot])
            def _(slot=slot):
                x_copy(1 - slot, v).wait_recv()

        left = chx[edge[0], edge[1]]
        for q in range(ny // 4):
            columns = [
                column(*split(jnp.concatenate([xrecv[slot, v, 2 * q + b] for slot in range(2)], axis=0)))
                for b in range(2)
            ]
            lined = turned[v, q]
            full = dot(left, jnp.concatenate([lined, lined, jnp.concatenate(columns, axis=1)], axis=0))
            for b in range(2):
                lanes = slice(b * nz, (b + 1) * nz)
                to_rows = pl.ds((4 * q + 2 * b) * nx, 2 * nx)
                tx[v, to_rows] = full[: 2 * nx, lanes]
                fx[v, to_rows] = full[2 * nx :, lanes]

    combine(0)
    for c in range(1, chunks):
        y_fix(c)
        combine(c)

    for slot in range(2):
        for c in range(chunks):

            @pl.when(has[2 + slot])
            def _(slot=slot, c=c):
                y_copy(slot, c).wait_send()

        for v in range(variables):

            @pl.when(has[slot])
            def _(slot=slot, v=v):
                x_copy(slot, v).wait_send()

    for v in range(variables):
        z_copy(v).wait_send()


def finish(tendency, updated, tendency_hbm, updated_hbm, sem):
    writes = [
        pltpu.make_async_copy(src.at[v], dst.at[v], sem.at[k, v])
        for v in range(tendency.shape[0])
        for k, (src, dst) in enumerate(((tendency, tendency_hbm), (updated, updated_hbm)))
    ]
    for write in writes:
        write.start()
    for write in writes:
        write.wait()


def on_device(counts, adjoint, base_density, base_velocity, base_pressure):
    variables, nx, ny, nz = adjoint.shape
    chunks = 3
    rows = nx * ny
    operators = tables(nx, ny, nz)
    field = (variables, rows, nz)
    y_shape = (2, chunks, variables, 8 * RANK, nz)
    x_shape = (2, variables, ny // 2, 2 * RANK, nz)
    dma = pltpu.SemaphoreType.DMA
    hbm = pl.BlockSpec(memory_space=pl.ANY)
    whole = pltpu.VMEM(field, F32)
    whole_low = pltpu.VMEM(field, BF16)
    cells = pltpu.VMEM((rows, nz), F32)
    tendency, updated = pl.pallas_call(
        functools.partial(kernel, counts),
        out_shape=[pltpu.VMEM(field, F32)] * 2,
        in_specs=[hbm] * 10,
        out_specs=[pl.BlockSpec(memory_space=pltpu.VMEM)] * 2,
        scratch_shapes=[
            whole,
            cells,
            pltpu.VMEM((3, rows, nz), F32),
            cells,
            *[pltpu.VMEM(m.shape, BF16) for m in operators],
            whole_low,
            whole_low,
            pltpu.VMEM((variables, ny // 4, 4 * nx, 2 * nz), BF16),
            whole,
            pltpu.VMEM(y_shape, F32),
            pltpu.VMEM(y_shape, F32),
            pltpu.VMEM(x_shape, F32),
            pltpu.VMEM(x_shape, F32),
            whole,
            whole,
            whole,
            whole,
            whole,
            cells,
            cells,
            dma((chunks,)),
            dma((9,)),
            dma((2, chunks)),
            dma((2, chunks)),
            dma((2, variables)),
            dma((2, variables)),
            dma((variables,)),
            dma((variables,)),
        ],
        compiler_params=pltpu.CompilerParams(
            collective_id=0, has_side_effects=True, vmem_limit_bytes=32 << 20
        ),
        name="adjoint_step",
    )(
        *[
            pltpu.with_memory_space_constraint(jnp.asarray(x), pltpu.HBM)
            for x in (
                adjoint.reshape(field),
                base_density.reshape(rows, nz),
                base_velocity.reshape(3, rows, nz),
                base_pressure.reshape(rows, nz),
                *operators,
            )
        ]
    )
    tendency, updated = pl.pallas_call(
        finish,
        out_shape=[jax.ShapeDtypeStruct(field, F32)] * 2,
        in_specs=[pl.BlockSpec(memory_space=pltpu.VMEM)] * 2,
        out_specs=[hbm] * 2,
        scratch_shapes=[dma((2, variables))],
        compiler_params=pltpu.CompilerParams(vmem_limit_bytes=16 << 20),
        name="finish",
    )(*[pltpu.with_memory_space_constraint(x, pltpu.VMEM) for x in (tendency, updated)])
    return tendency.reshape(adjoint.shape), updated.reshape(adjoint.shape)


def solution(mesh):
    placed = (
        P(None, "gx", "gy", "gz"),
        P("gx", "gy", "gz"),
        P(None, "gx", "gy", "gz"),
        P("gx", "gy", "gz"),
    )
    return jax.shard_map(
        functools.partial(on_device, (mesh.shape["gx"], mesh.shape["gy"])),
        mesh=mesh,
        in_specs=placed,
        out_specs=(P(None, "gx", "gy", "gz"), P(None, "gx", "gy", "gz")),
        check_vma=False,
    )
```

```python
import functools

import jax
import jax.numpy as jnp
import numpy as np
from jax import lax
from jax.experimental import pallas as pl
from jax.experimental.pallas import tpu as pltpu
from jax.sharding import PartitionSpec as P

GAMMA_LESS = 0.4
RATIO = 1.0 / 3.0
COEF_NEAR = 7.0 / 9.0
COEF_FAR = 1.0 / 36.0
RANK = 4
THIN = True
SENT = 24 if THIN else 32
EDGE = 16
F32 = jnp.float32
BF16 = jnp.bfloat16


def derivative(total, periodic):
    eye = np.eye(total)
    if periodic:
        up1, lo1, up2, lo2 = (np.roll(eye, s, axis=1) for s in (1, -1, 2, -2))
    else:
        up1, lo1, up2, lo2 = (np.eye(total, k=s) for s in (1, -1, 2, -2))
    banded = eye + RATIO * (up1 + lo1)
    stencil = COEF_NEAR * (up1 - lo1) + COEF_FAR * (up2 - lo2)
    return -stencil @ np.linalg.inv(banded)


def stacked(matrix, rows, cols):
    return np.vstack([(matrix @ matrix)[rows, cols], -2.0 * matrix[rows, cols]])


def line_factors(block, thin):
    long = derivative(9 * block, False)
    near = derivative(4 * block, False)
    own = slice(4 * block, 5 * block)
    local = stacked(long, own, own)
    sides = []
    for beside, edge in (
        (slice(3 * block, 4 * block), slice(0, block)),
        (slice(5 * block, 6 * block), slice(3 * block, 4 * block)),
    ):
        basis, size, functional = np.linalg.svd(stacked(long, own, beside))
        basis, size, functional = basis[:, :RANK], size[:RANK], functional[:RANK]
        end = (basis, basis.T @ (stacked(near, edge, edge) - local))
        if thin:
            flat = functional.sum(axis=1)
            unseen = np.eye(RANK)[-1] - flat * flat[-1] / (flat @ flat)
            left_out = unseen / size**2
            left_out /= unseen @ left_out
            kept = np.linalg.svd(left_out[None])[2][1:].T
            basis, mixed = np.linalg.qr((basis * size) @ (np.eye(RANK) - np.outer(left_out, unseen)) @ kept)
            sides.append(((basis, mixed @ kept.T @ functional), end))
        else:
            sides.append(((basis, size[:, None] * functional), end))
    return local, sides


def four(matrix):
    high = matrix.astype(np.float32).astype(BF16)
    low = (matrix - high.astype(np.float64)).astype(np.float32).astype(BF16)
    return np.concatenate([high, high, low, low], axis=1)


def direction(block, lines, thin):
    local, sides = line_factors(block, thin)
    eye = np.eye(lines)
    order = [(slice(0, 2), slice(2, 3), slice(2, 3) if thin else slice(3, 4)), (slice(0, 2), slice(2, 3), slice(3, 4))]
    state = np.stack(
        [
            np.stack(
                [
                    four(np.vstack([np.kron(eye, factors[1][part]) for part in order[end]]))
                    for end, factors in enumerate(pair)
                ]
            )
            for pair in ((sides[1][0], sides[0][1]), (sides[0][0], sides[1][1]))
        ]
    )
    whole = four(np.vstack([np.kron(eye, local[:block]), np.kron(eye, local[block:])]))

    def gained(ends):
        return np.vstack(
            [
                np.hstack(
                    [np.kron(eye, side[end][0][half, part]) for side, end in zip(sides, ends) for part in order[end]]
                )
                for half in (slice(0, block), slice(block, None))
            ]
        )

    change = np.stack([np.stack([four(gained((a, b))) for b in range(2)]) for a in range(2)])
    both = np.concatenate([np.broadcast_to(whole, change.shape[:2] + whole.shape), change], axis=-1)
    return state, whole, change, both


def span_table(nz):
    span = derivative(2 * nz, True)
    both = np.hstack([(span @ span)[:nz].T, -2.0 * span[:nz].T])
    high = both.astype(np.float32).astype(BF16)
    low = (both - high.astype(np.float64)).astype(np.float32).astype(BF16)
    first, last = [nz + k for k in range(EDGE)], [2 * nz - EDGE + k for k in range(EDGE)]
    rest = np.zeros((nz - 6 * EDGE, 2 * nz), BF16)
    second = np.concatenate(
        [low[:nz], high[first], high[last], high[first], low[last], low[first], rest, high[last]], axis=0
    )
    return np.stack([np.concatenate([high[:nz], high[:nz]], axis=0), second])


@functools.lru_cache(maxsize=None)
def tables(nx, ny, nz):
    state_y, local_y, change_y, _ = direction(ny, 4, THIN)
    state_x, _, _, both_x = direction(nx, 2, THIN)
    return state_y, local_y, change_y, state_x, both_x, span_table(nz)


def split(value):
    high = value.astype(BF16)
    return high, (value - high.astype(F32)).astype(BF16)


def column(high, low):
    return jnp.concatenate([high, low, high, low], axis=0)


def dot(a, b):
    return jnp.dot(a, b, preferred_element_type=F32)


def pull(first, d, speed, square, enthalpy):
    head = first[1] * speed[0] + first[2] * speed[1] + first[3] * speed[2] + enthalpy * first[4]
    push = GAMMA_LESS * (first[1 + d] + speed[d] * first[4])
    result = [square * push - speed[d] * head]
    for i in range(3):
        term = speed[d] * first[1 + i] - speed[i] * push
        result.append(term + (first[0] + head) if i == d else term)
    result.append(speed[d] * first[4] + push)
    return result


def pull_two(g, k, speed, square, enthalpy):
    head_g = g[1] * speed[0] + g[2] * speed[1] + g[3] * speed[2] + enthalpy * g[4]
    head_k = k[1] * speed[0] + k[2] * speed[1] + k[3] * speed[2] + enthalpy * k[4]
    energy = speed[0] * g[4] + speed[1] * k[4]
    push = GAMMA_LESS * ((g[1] + k[2]) + energy)
    return [
        square * push - (speed[0] * head_g + speed[1] * head_k),
        (speed[0] * (g[1] - push) + speed[1] * k[1]) + (g[0] + head_g),
        (speed[0] * g[2] + speed[1] * (k[2] - push)) + (k[0] + head_k),
        speed[0] * g[3] + speed[1] * k[3] - speed[2] * push,
        energy + push,
    ]


def kernel(
    counts,
    adj_hbm, rho_hbm, vel_hbm, pre_hbm, sty_hbm, loy_hbm, chy_hbm, stx_hbm, chx_hbm, spn_hbm,
    tendency, updated,
    adj, rho, vel, pre, sty, loy, chy, stx, chx, spn,
    highs, lows, turned, other, ysend, yrecv, xsend, xrecv, twice, fy, tx, fx, tz, squares, heats,
    adj_sem, in_sem, ys_sem, yr_sem, xs_sem, xr_sem, zs_sem, zr_sem,
):
    gx, gy, gz = (lax.axis_index(n) for n in ("gx", "gy", "gz"))
    n_gx, n_gy = counts
    variables, rows_all, nz = adj.shape
    chunks = ysend.shape[1]
    rows_c = rows_all // chunks
    half = rows_c // 2
    ny = 16
    nx = rows_all // ny

    pieces = [
        pltpu.make_async_copy(
            adj_hbm.at[:, pl.ds(c * rows_c, rows_c)], adj.at[:, pl.ds(c * rows_c, rows_c)], adj_sem.at[c]
        )
        for c in range(chunks)
    ]
    loads = [
        pltpu.make_async_copy(src, dst, in_sem.at[k])
        for k, (src, dst) in enumerate(
            ((sty_hbm, sty), (stx_hbm, stx), (loy_hbm, loy), (spn_hbm, spn),
             (rho_hbm, rho), (vel_hbm, vel), (pre_hbm, pre), (chx_hbm, chx), (chy_hbm, chy))
        )
    ]
    pieces[0].start()
    loads[0].start()

    has = (gx > 0, gx < n_gx - 1, gy > 0, gy < n_gy - 1)
    edge = tuple(jnp.where(there, 0, 1) for there in has)
    to = ({"gx": gx - 1}, {"gx": gx + 1}, {"gy": gy - 1}, {"gy": gy + 1})
    partner = {"gz": 1 - gz}
    lane = lax.broadcasted_iota(jnp.int32, (rows_all, nz), 1)
    upper = lax.broadcasted_iota(jnp.int32, (8, nz), 0) < 4
    own_rest = tuple(jnp.logical_not(there) if THIN else True for there in has)
    sub = lax.broadcasted_iota(jnp.int32, (8, nz), 0)

    def pack(found):
        ahead = [pltpu.roll(f, 4, 0) if h % 2 else f for h, f in enumerate(found)]
        pairs = [jnp.where(sub < 4, ahead[2 * p], ahead[2 * p + 1]) for p in range(4)]
        thirds = [
            jnp.where(
                sub < 4,
                jnp.where(sub < 2, ahead[g + 1], ahead[g + 3]),
                jnp.where(sub < 6, ahead[g], ahead[g + 2]),
            )
            for g in (0, 4)
        ]
        return pairs + thirds

    def unpack(slot, v, h):
        low = 2 * ((h % 4) // 2) + 4 * (1 - h % 2)
        mine = sub >= 4 if h % 2 else sub < 4
        third = jnp.where((sub >= low) & (sub < low + 2), xrecv[slot, v, 4 + h // 4], 0.0)
        got = jnp.where(mine, xrecv[slot, v, h // 2], third)
        if h % 2:
            got = pltpu.roll(got, 4, 0)
        return jnp.where(own_rest[slot], xrecv[slot, v, h], got)

    barrier = pltpu.get_barrier_semaphore()
    for there, where in zip(has, to):

        @pl.when(there)
        def _(where=where):
            pl.semaphore_signal(barrier, inc=1, device_id=where, device_id_type=pl.DeviceIdType.MESH)

    pl.semaphore_signal(barrier, inc=1, device_id=partner, device_id_type=pl.DeviceIdType.MESH)
    for load in pieces[1:] + loads[1:]:
        load.start()
    neighbours = sum(jnp.where(there, 1, 0) for there in has) + 1

    def remote(src, dst, send, recv, where):
        return pltpu.make_async_remote_copy(
            src_ref=src, dst_ref=dst, send_sem=send, recv_sem=recv,
            device_id=where, device_id_type=pl.DeviceIdType.MESH,
        )

    def y_copy(slot, c):
        return remote(
            ysend.at[slot, c, :, pl.ds(0, SENT)], yrecv.at[1 - slot, c, :, pl.ds(0, SENT)], ys_sem.at[slot, c], yr_sem.at[1 - slot, c], to[2 + slot]
        )

    def x_copy(slot, v):
        return remote(
            xsend.at[slot, v, pl.ds(0, 6)], xrecv.at[1 - slot, v, pl.ds(0, 6)], xs_sem.at[slot, v], xr_sem.at[1 - slot, v], to[slot]
        )

    def z_copy(v):
        return remote(adj_hbm.at[v], other.at[v], zs_sem.at[v], zr_sem.at[v], partner)

    def y_part(c):
        rows = pl.ds(c * rows_c, rows_c)
        left = jnp.concatenate([sty[0, edge[2]], sty[1, edge[3]]], axis=0)
        k = sty.shape[2]
        for v in range(variables):
            high, low = split(adj[v, rows])
            highs[v, rows] = high
            lows[v, rows] = low
            right = jnp.concatenate([column(high[:half], low[:half]), column(high[half:], low[half:])], axis=1)
            full = dot(left, right)
            for slot in range(2):
                pair, rest = full[slot * k : slot * k + 8], full[slot * k + 8 : (slot + 1) * k]
                ysend[slot, c, v, :8] = pair[:, :nz]
                ysend[slot, c, v, 8:16] = pair[:, nz:]
                ysend[slot, c, v, 16:24] = jnp.where(upper | own_rest[2 + slot], rest[:, :nz], rest[:, nz:])
                ysend[slot, c, v, 24:] = rest[:, nz:]
        if c == 0:
            pl.semaphore_wait(barrier, neighbours)
        for slot in range(2):

            @pl.when(has[2 + slot])
            def _(slot=slot):
                y_copy(slot, c).start()

            @pl.when(jnp.logical_not(has[2 + slot]))
            def _(slot=slot):
                yrecv[slot, c] = ysend[slot, c]

    pieces[0].wait()
    loads[0].wait()
    y_part(0)
    for v in range(variables):
        z_copy(v).start()
    for c in range(1, chunks):
        pieces[c].wait()
    loads[1].wait()
    loads[2].wait()

    @pl.loop(0, variables)
    def _(v):
        found = ([], [])
        left = jnp.concatenate([stx[0, edge[0]], stx[1, edge[1]]], axis=0)
        k = stx.shape[2]
        for q in range(ny // 4):
            halves = []
            for b in range(2):
                lines = [adj[v, pl.ds(4 * q + 2 * b + j, nx, stride=ny)] for j in range(2)]
                halves.append(jnp.concatenate(split(jnp.concatenate(lines, axis=0)), axis=0))
            lined = jnp.concatenate(halves, axis=1)
            turned[v, q] = lined
            full = dot(left, jnp.concatenate([lined, lined], axis=0))
            for b in range(2):
                for slot in range(2):
                    found[slot].append(full[slot * k : (slot + 1) * k, b * nz : (b + 1) * nz])
        for slot in range(2):
            for at, packed in enumerate(pack(found[slot])):
                xsend[slot, v, at] = jnp.where(own_rest[slot], found[slot][at], packed)
            for at in range(6, 8):
                xsend[slot, v, at] = found[slot][at]
        for slot in range(2):

            @pl.when(has[slot])
            def _(slot=slot):
                x_copy(slot, v).start()

            @pl.when(jnp.logical_not(has[slot]))
            def _(slot=slot):
                xrecv[slot, v] = xsend[slot, v]

    for c in range(1, chunks):
        y_part(c)

    for load in loads[3:]:
        load.wait()
    for c in range(chunks):
        rows = pl.ds(c * rows_c, rows_c)
        for v in range(variables):
            high, low = highs[v, rows], lows[v, rows]
            full = dot(
                loy[...],
                jnp.concatenate([column(high[:half], low[:half]), column(high[half:], low[half:])], axis=1),
            )
            for b in range(2):
                lanes = slice(b * nz, (b + 1) * nz)
                to_rows = pl.ds(c * rows_c + b * half, half)
                twice[v, to_rows] = full[:half, lanes]
                fy[v, to_rows] = full[half:, lanes]

    for v in range(variables):
        z_copy(v).wait_recv()

    for v in range(variables):
        theirs = other[v]
        at_low = pltpu.roll(theirs, 2 * EDGE, 1)
        at_low = at_low - at_low.astype(BF16).astype(F32)
        ends = jnp.where((lane >= EDGE) & (lane < 3 * EDGE), at_low, theirs)
        ends = jnp.where((lane >= 3 * EDGE) & (lane < 5 * EDGE), pltpu.roll(theirs, 4 * EDGE, 1), ends).astype(BF16)
        high = highs[v]
        full = dot(jnp.concatenate([high, lows[v]], axis=1), spn[0]) + dot(
            jnp.concatenate([high, ends], axis=1), spn[1]
        )
        tz[v] = full[:, :nz]
        other[v] = full[:, nz:]

    tile = 2 * ny

    @pl.loop(0, rows_all // tile)
    def _(t):
        at = pl.ds(pl.multiple_of(t * tile, tile), tile)
        speed = [vel[d, at] for d in range(3)]
        square = 0.5 * (speed[0] * speed[0] + speed[1] * speed[1] + speed[2] * speed[2])
        heat = (1.0 + 1.0 / GAMMA_LESS) * pre[at] / rho[at] + square
        squares[at] = square
        heats[at] = heat
        gained = pull([other[v, at] for v in range(5)], 2, speed, square, heat)
        for v in range(5):
            tz[v, at] += gained[v]

    def y_fix(c):
        rows = pl.ds(c * rows_c, rows_c)
        for slot in range(2):

            @pl.when(has[2 + slot])
            def _(slot=slot):
                y_copy(1 - slot, c).wait_recv()

        for v in range(variables):
            parts = ([], [])
            for slot in range(2):
                rest, last = yrecv[slot, c, v, 16:24], yrecv[slot, c, v, 24:]
                parts[0].extend([yrecv[slot, c, v, :8], jnp.where(upper | own_rest[2 + slot], rest, 0.0)])
                parts[1].extend(
                    [yrecv[slot, c, v, 8:16], jnp.where(own_rest[2 + slot], last, jnp.where(upper, 0.0, rest))]
                )
            columns = [column(*split(jnp.concatenate(part, axis=0))) for part in parts]
            full = dot(chy[edge[2], edge[3]], jnp.concatenate(columns, axis=1))
            for b in range(2):
                lanes = slice(b * nz, (b + 1) * nz)
                to_rows = pl.ds(c * rows_c + b * half, half)
                twice[v, to_rows] += full[:half, lanes]
                fy[v, to_rows] += full[half:, lanes]

    def take_y(c):
        @pl.loop(0, rows_c // tile)
        def _(t):
            at = pl.ds(pl.multiple_of(c * rows_c + t * tile, tile), tile)
            speed = [vel[d, at] for d in range(3)]
            gain = pull([fy[v, at] for v in range(5)], 1, speed, squares[at], heats[at])
            for v in range(5):
                tz[v, at] += twice[v, at] + gain[v]

    def take_x(c):
        @pl.loop(0, rows_c // tile)
        def _(t):
            at = pl.ds(pl.multiple_of(c * rows_c + t * tile, tile), tile)
            first_line = c * (rows_c // ny) + t * (tile // ny)

            def natural(ref, v):
                return jnp.concatenate(
                    [ref[v, pl.ds(first_line + j, ny, stride=nx)] for j in range(tile // ny)], axis=0
                )

            speed = [vel[d, at] for d in range(3)]
            gain = pull([natural(fx, v) for v in range(5)], 0, speed, squares[at], heats[at])
            for v in range(5):
                total = (tz[v, at] + natural(tx, v)) + gain[v]
                tendency[v, at] = 0.5 * total
                updated[v, at] = adj[v, at] + 0.25 * total

    def combine(c):
        @pl.loop(0, rows_c // tile)
        def _(t):
            at = pl.ds(pl.multiple_of(c * rows_c + t * tile, tile), tile)
            first_line = c * (rows_c // ny) + t * (tile // ny)

            def natural(ref, v):
                return jnp.concatenate(
                    [ref[v, pl.ds(first_line + j, ny, stride=nx)] for j in range(tile // ny)], axis=0
                )

            speed = [vel[d, at] for d in range(3)]
            square, heat = squares[at], heats[at]
            gain = pull_two(
                [natural(fx, v) for v in range(5)], [fy[v, at] for v in range(5)], speed, square, heat
            )
            for v in range(5):
                total = (twice[v, at] + natural(tx, v)) + (tz[v, at] + gain[v])
                tendency[v, at] = 0.5 * total
                updated[v, at] = adj[v, at] + 0.25 * total

    y_fix(0)
    take_y(0)

    @pl.loop(0, variables)
    def _(v):
        for slot in range(2):

            @pl.when(has[slot])
            def _(slot=slot):
                x_copy(1 - slot, v).wait_recv()

        left = chx[edge[0], edge[1]]
        for q in range(ny // 4):
            columns = [
                column(*split(jnp.concatenate([unpack(slot, v, 2 * q + b) for slot in range(2)], axis=0)))
                for b in range(2)
            ]
            lined = turned[v, q]
            full = dot(left, jnp.concatenate([lined, lined, jnp.concatenate(columns, axis=1)], axis=0))
            for b in range(2):
                lanes = slice(b * nz, (b + 1) * nz)
                to_rows = pl.ds((4 * q + 2 * b) * nx, 2 * nx)
                tx[v, to_rows] = full[: 2 * nx, lanes]
                fx[v, to_rows] = full[2 * nx :, lanes]

    take_x(0)
    for c in range(1, chunks):
        y_fix(c)
        combine(c)

    for slot in range(2):
        for c in range(chunks):

            @pl.when(has[2 + slot])
            def _(slot=slot, c=c):
                y_copy(slot, c).wait_send()

        for v in range(variables):

            @pl.when(has[slot])
            def _(slot=slot, v=v):
                x_copy(slot, v).wait_send()

    for v in range(variables):
        z_copy(v).wait_send()


def finish(tendency, updated, tendency_hbm, updated_hbm, sem):
    writes = [
        pltpu.make_async_copy(src.at[v], dst.at[v], sem.at[k, v])
        for v in range(tendency.shape[0])
        for k, (src, dst) in enumerate(((tendency, tendency_hbm), (updated, updated_hbm)))
    ]
    for write in writes:
        write.start()
    for write in writes:
        write.wait()


def on_device(counts, adjoint, base_density, base_velocity, base_pressure):
    variables, nx, ny, nz = adjoint.shape
    chunks = 3
    rows = nx * ny
    operators = tables(nx, ny, nz)
    field = (variables, rows, nz)
    y_shape = (2, chunks, variables, 8 * RANK, nz)
    x_shape = (2, variables, ny // 2, 2 * RANK, nz)
    dma = pltpu.SemaphoreType.DMA
    hbm = pl.BlockSpec(memory_space=pl.ANY)
    whole = pltpu.VMEM(field, F32)
    whole_low = pltpu.VMEM(field, BF16)
    cells = pltpu.VMEM((rows, nz), F32)
    tendency, updated = pl.pallas_call(
        functools.partial(kernel, counts),
        out_shape=[pltpu.VMEM(field, F32)] * 2,
        in_specs=[hbm] * 10,
        out_specs=[pl.BlockSpec(memory_space=pltpu.VMEM)] * 2,
        scratch_shapes=[
            whole,
            cells,
            pltpu.VMEM((3, rows, nz), F32),
            cells,
            *[pltpu.VMEM(m.shape, BF16) for m in operators],
            whole_low,
            whole_low,
            pltpu.VMEM((variables, ny // 4, 4 * nx, 2 * nz), BF16),
            whole,
            pltpu.VMEM(y_shape, F32),
            pltpu.VMEM(y_shape, F32),
            pltpu.VMEM(x_shape, F32),
            pltpu.VMEM(x_shape, F32),
            whole,
            whole,
            whole,
            whole,
            whole,
            cells,
            cells,
            dma((chunks,)),
            dma((9,)),
            dma((2, chunks)),
            dma((2, chunks)),
            dma((2, variables)),
            dma((2, variables)),
            dma((variables,)),
            dma((variables,)),
        ],
        compiler_params=pltpu.CompilerParams(
            collective_id=0, has_side_effects=True, vmem_limit_bytes=32 << 20
        ),
        name="adjoint_step",
    )(
        *[
            pltpu.with_memory_space_constraint(jnp.asarray(x), pltpu.HBM)
            for x in (
                adjoint.reshape(field),
                base_density.reshape(rows, nz),
                base_velocity.reshape(3, rows, nz),
                base_pressure.reshape(rows, nz),
                *operators,
            )
        ]
    )
    tendency, updated = pl.pallas_call(
        finish,
        out_shape=[jax.ShapeDtypeStruct(field, F32)] * 2,
        in_specs=[pl.BlockSpec(memory_space=pltpu.VMEM)] * 2,
        out_specs=[hbm] * 2,
        scratch_shapes=[dma((2, variables))],
        compiler_params=pltpu.CompilerParams(vmem_limit_bytes=16 << 20),
        name="finish",
    )(*[pltpu.with_memory_space_constraint(x, pltpu.VMEM) for x in (tendency, updated)])
    return tendency.reshape(adjoint.shape), updated.reshape(adjoint.shape)


def solution(mesh):
    placed = (
        P(None, "gx", "gy", "gz"),
        P("gx", "gy", "gz"),
        P(None, "gx", "gy", "gz"),
        P("gx", "gy", "gz"),
    )
    return jax.shard_map(
        functools.partial(on_device, (mesh.shape["gx"], mesh.shape["gy"])),
        mesh=mesh,
        in_specs=placed,
        out_specs=(P(None, "gx", "gy", "gz"), P(None, "gx", "gy", "gz")),
        check_vma=False,
    )
```

```python
import functools

import jax
import jax.numpy as jnp
import numpy as np
from jax import lax
from jax.experimental import pallas as pl
from jax.experimental.pallas import tpu as pltpu
from jax.sharding import PartitionSpec as P

GAMMA_LESS = 0.4
RATIO = 1.0 / 3.0
COEF_NEAR = 7.0 / 9.0
COEF_FAR = 1.0 / 36.0
RANK = 4
THIN = True
SENT = 24 if THIN else 32
EDGE = 16
F32 = jnp.float32
BF16 = jnp.bfloat16


def derivative(total, periodic):
    eye = np.eye(total)
    if periodic:
        up1, lo1, up2, lo2 = (np.roll(eye, s, axis=1) for s in (1, -1, 2, -2))
    else:
        up1, lo1, up2, lo2 = (np.eye(total, k=s) for s in (1, -1, 2, -2))
    banded = eye + RATIO * (up1 + lo1)
    stencil = COEF_NEAR * (up1 - lo1) + COEF_FAR * (up2 - lo2)
    return -stencil @ np.linalg.inv(banded)


def stacked(matrix, rows, cols):
    return np.vstack([(matrix @ matrix)[rows, cols], -2.0 * matrix[rows, cols]])


def line_factors(block, thin):
    long = derivative(9 * block, False)
    near = derivative(4 * block, False)
    own = slice(4 * block, 5 * block)
    local = stacked(long, own, own)
    sides = []
    for beside, edge in (
        (slice(3 * block, 4 * block), slice(0, block)),
        (slice(5 * block, 6 * block), slice(3 * block, 4 * block)),
    ):
        basis, size, functional = np.linalg.svd(stacked(long, own, beside))
        basis, size, functional = basis[:, :RANK], size[:RANK], functional[:RANK]
        end = (basis, basis.T @ (stacked(near, edge, edge) - local))
        if thin:
            flat = functional.sum(axis=1)
            unseen = np.eye(RANK)[-1] - flat * flat[-1] / (flat @ flat)
            left_out = unseen / size**2
            left_out /= unseen @ left_out
            kept = np.linalg.svd(left_out[None])[2][1:].T
            basis, mixed = np.linalg.qr((basis * size) @ (np.eye(RANK) - np.outer(left_out, unseen)) @ kept)
            sides.append(((basis, mixed @ kept.T @ functional), end))
        else:
            sides.append(((basis, size[:, None] * functional), end))
    return local, sides


def four(matrix):
    high = matrix.astype(np.float32).astype(BF16)
    low = (matrix - high.astype(np.float64)).astype(np.float32).astype(BF16)
    return np.concatenate([high, high, low, low], axis=1)


def direction(block, lines, thin):
    local, sides = line_factors(block, thin)
    eye = np.eye(lines)
    order = [(slice(0, 2), slice(2, 3), slice(2, 3) if thin else slice(3, 4)), (slice(0, 2), slice(2, 3), slice(3, 4))]
    state = np.stack(
        [
            np.stack(
                [
                    four(np.vstack([np.kron(eye, factors[1][part]) for part in order[end]]))
                    for end, factors in enumerate(pair)
                ]
            )
            for pair in ((sides[1][0], sides[0][1]), (sides[0][0], sides[1][1]))
        ]
    )
    whole = four(np.vstack([np.kron(eye, local[:block]), np.kron(eye, local[block:])]))

    def gained(ends):
        return np.vstack(
            [
                np.hstack(
                    [np.kron(eye, side[end][0][half, part]) for side, end in zip(sides, ends) for part in order[end]]
                )
                for half in (slice(0, block), slice(block, None))
            ]
        )

    change = np.stack([np.stack([four(gained((a, b))) for b in range(2)]) for a in range(2)])
    both = np.concatenate([np.broadcast_to(whole, change.shape[:2] + whole.shape), change], axis=-1)
    return state, whole, change, both


def span_table(nz):
    span = derivative(2 * nz, True)
    both = np.hstack([(span @ span)[:nz].T, -2.0 * span[:nz].T])
    high = both.astype(np.float32).astype(BF16)
    low = (both - high.astype(np.float64)).astype(np.float32).astype(BF16)
    first, last = [nz + k for k in range(EDGE)], [2 * nz - EDGE + k for k in range(EDGE)]
    rest = np.zeros((nz - 6 * EDGE, 2 * nz), BF16)
    second = np.concatenate(
        [low[:nz], high[first], high[last], high[first], low[last], low[first], rest, high[last]], axis=0
    )
    return np.stack([np.concatenate([high[:nz], high[:nz]], axis=0), second])


@functools.lru_cache(maxsize=None)
def tables(nx, ny, nz):
    state_y, local_y, change_y, _ = direction(ny, 4, THIN)
    state_x, _, _, both_x = direction(nx, 2, THIN)
    return state_y, local_y, change_y, state_x, both_x, span_table(nz)


def split(value):
    high = value.astype(BF16)
    return high, (value - high.astype(F32)).astype(BF16)


def column(high, low):
    return jnp.concatenate([high, low, high, low], axis=0)


def dot(a, b):
    return jnp.dot(a, b, preferred_element_type=F32)


def pull(first, d, speed, square, enthalpy):
    head = first[1] * speed[0] + first[2] * speed[1] + first[3] * speed[2] + enthalpy * first[4]
    push = GAMMA_LESS * (first[1 + d] + speed[d] * first[4])
    result = [square * push - speed[d] * head]
    for i in range(3):
        term = speed[d] * first[1 + i] - speed[i] * push
        result.append(term + (first[0] + head) if i == d else term)
    result.append(speed[d] * first[4] + push)
    return result


def pull_two(g, k, speed, square, enthalpy):
    head_g = g[1] * speed[0] + g[2] * speed[1] + g[3] * speed[2] + enthalpy * g[4]
    head_k = k[1] * speed[0] + k[2] * speed[1] + k[3] * speed[2] + enthalpy * k[4]
    energy = speed[0] * g[4] + speed[1] * k[4]
    push = GAMMA_LESS * ((g[1] + k[2]) + energy)
    return [
        square * push - (speed[0] * head_g + speed[1] * head_k),
        (speed[0] * (g[1] - push) + speed[1] * k[1]) + (g[0] + head_g),
        (speed[0] * g[2] + speed[1] * (k[2] - push)) + (k[0] + head_k),
        speed[0] * g[3] + speed[1] * k[3] - speed[2] * push,
        energy + push,
    ]


def kernel(
    counts,
    adj_hbm, rho_hbm, vel_hbm, pre_hbm, sty_hbm, loy_hbm, chy_hbm, stx_hbm, chx_hbm, spn_hbm,
    tendency, updated,
    adj, rho, vel, pre, sty, loy, chy, stx, chx, spn,
    highs, lows, turned, other, ysend, yrecv, xsend, xrecv, twice, fy, tx, fx, tz, squares, heats,
    adj_sem, in_sem, ys_sem, yr_sem, xs_sem, xr_sem, zs_sem, zr_sem,
):
    gx, gy, gz = (lax.axis_index(n) for n in ("gx", "gy", "gz"))
    n_gx, n_gy = counts
    variables, rows_all, nz = adj.shape
    chunks = ysend.shape[1]
    rows_c = rows_all // chunks
    half = rows_c // 2
    ny = 16
    nx = rows_all // ny

    pieces = [
        pltpu.make_async_copy(
            adj_hbm.at[:, pl.ds(c * rows_c, rows_c)], adj.at[:, pl.ds(c * rows_c, rows_c)], adj_sem.at[c]
        )
        for c in range(chunks)
    ]
    loads = [
        pltpu.make_async_copy(src, dst, in_sem.at[k])
        for k, (src, dst) in enumerate(
            ((sty_hbm, sty), (stx_hbm, stx), (loy_hbm, loy), (spn_hbm, spn),
             (rho_hbm, rho), (vel_hbm, vel), (pre_hbm, pre), (chx_hbm, chx), (chy_hbm, chy))
        )
    ]
    pieces[0].start()
    loads[0].start()

    has = (gx > 0, gx < n_gx - 1, gy > 0, gy < n_gy - 1)
    edge = tuple(jnp.where(there, 0, 1) for there in has)
    to = ({"gx": gx - 1}, {"gx": gx + 1}, {"gy": gy - 1}, {"gy": gy + 1})
    partner = {"gz": 1 - gz}
    lane = lax.broadcasted_iota(jnp.int32, (rows_all, nz), 1)
    upper = lax.broadcasted_iota(jnp.int32, (8, nz), 0) < 4
    own_rest = tuple(jnp.logical_not(there) if THIN else True for there in has)
    sub = lax.broadcasted_iota(jnp.int32, (8, nz), 0)

    def pack(found):
        ahead = [pltpu.roll(f, 4, 0) if h % 2 else f for h, f in enumerate(found)]
        pairs = [jnp.where(sub < 4, ahead[2 * p], ahead[2 * p + 1]) for p in range(4)]
        thirds = [
            jnp.where(
                sub < 4,
                jnp.where(sub < 2, ahead[g + 1], ahead[g + 3]),
                jnp.where(sub < 6, ahead[g], ahead[g + 2]),
            )
            for g in (0, 4)
        ]
        return pairs + thirds

    def unpack(slot, v, h):
        low = 2 * ((h % 4) // 2) + 4 * (1 - h % 2)
        mine = sub >= 4 if h % 2 else sub < 4
        third = jnp.where((sub >= low) & (sub < low + 2), xrecv[slot, v, 4 + h // 4], 0.0)
        got = jnp.where(mine, xrecv[slot, v, h // 2], third)
        if h % 2:
            got = pltpu.roll(got, 4, 0)
        return jnp.where(own_rest[slot], xrecv[slot, v, h], got)

    barrier = pltpu.get_barrier_semaphore()
    for there, where in zip(has, to):

        @pl.when(there)
        def _(where=where):
            pl.semaphore_signal(barrier, inc=1, device_id=where, device_id_type=pl.DeviceIdType.MESH)

    pl.semaphore_signal(barrier, inc=1, device_id=partner, device_id_type=pl.DeviceIdType.MESH)
    for load in pieces[1:] + loads[1:]:
        load.start()
    neighbours = sum(jnp.where(there, 1, 0) for there in has) + 1

    def remote(src, dst, send, recv, where):
        return pltpu.make_async_remote_copy(
            src_ref=src, dst_ref=dst, send_sem=send, recv_sem=recv,
            device_id=where, device_id_type=pl.DeviceIdType.MESH,
        )

    def y_copy(slot, c):
        return remote(
            ysend.at[slot, c, :, pl.ds(0, SENT)], yrecv.at[1 - slot, c, :, pl.ds(0, SENT)], ys_sem.at[slot, c], yr_sem.at[1 - slot, c], to[2 + slot]
        )

    def x_copy(slot, v):
        return remote(
            xsend.at[slot, v, pl.ds(0, 6)], xrecv.at[1 - slot, v, pl.ds(0, 6)], xs_sem.at[slot, v], xr_sem.at[1 - slot, v], to[slot]
        )

    def z_copy(v):
        return remote(adj_hbm.at[v], other.at[v], zs_sem.at[v], zr_sem.at[v], partner)

    def y_part(c):
        rows = pl.ds(c * rows_c, rows_c)
        left = jnp.concatenate([sty[0, edge[2]], sty[1, edge[3]]], axis=0)
        k = sty.shape[2]
        for v in range(variables):
            high, low = split(adj[v, rows])
            highs[v, rows] = high
            lows[v, rows] = low
            right = jnp.concatenate([column(high[:half], low[:half]), column(high[half:], low[half:])], axis=1)
            full = dot(left, right)
            for slot in range(2):
                pair, rest = full[slot * k : slot * k + 8], full[slot * k + 8 : (slot + 1) * k]
                ysend[slot, c, v, :8] = pair[:, :nz]
                ysend[slot, c, v, 8:16] = pair[:, nz:]
                ysend[slot, c, v, 16:24] = jnp.where(upper | own_rest[2 + slot], rest[:, :nz], rest[:, nz:])
                ysend[slot, c, v, 24:] = rest[:, nz:]

    def y_send(c):
        for slot in range(2):

            @pl.when(has[2 + slot])
            def _(slot=slot):
                y_copy(slot, c).start()

            @pl.when(jnp.logical_not(has[2 + slot]))
            def _(slot=slot):
                yrecv[slot, c] = ysend[slot, c]

    pieces[0].wait()
    loads[0].wait()
    y_part(0)
    for c in range(1, chunks):
        pieces[c].wait()
    loads[1].wait()
    loads[2].wait()

    y_part(1)
    pl.semaphore_wait(barrier, neighbours)
    y_send(0)
    y_send(1)
    for v in range(variables):
        z_copy(v).start()
    @pl.loop(0, variables)
    def _(v):
        found = ([], [])
        left = jnp.concatenate([stx[0, edge[0]], stx[1, edge[1]]], axis=0)
        k = stx.shape[2]
        for q in range(ny // 4):
            halves = []
            for b in range(2):
                lines = [adj[v, pl.ds(4 * q + 2 * b + j, nx, stride=ny)] for j in range(2)]
                halves.append(jnp.concatenate(split(jnp.concatenate(lines, axis=0)), axis=0))
            lined = jnp.concatenate(halves, axis=1)
            turned[v, q] = lined
            full = dot(left, jnp.concatenate([lined, lined], axis=0))
            for b in range(2):
                for slot in range(2):
                    found[slot].append(full[slot * k : (slot + 1) * k, b * nz : (b + 1) * nz])
        for slot in range(2):
            for at, packed in enumerate(pack(found[slot])):
                xsend[slot, v, at] = jnp.where(own_rest[slot], found[slot][at], packed)
            for at in range(6, 8):
                xsend[slot, v, at] = found[slot][at]
        for slot in range(2):

            @pl.when(has[slot])
            def _(slot=slot):
                x_copy(slot, v).start()

            @pl.when(jnp.logical_not(has[slot]))
            def _(slot=slot):
                xrecv[slot, v] = xsend[slot, v]

    for c in range(2, chunks):
        y_part(c)
        y_send(c)

    for load in loads[3:]:
        load.wait()
    for c in range(chunks):
        rows = pl.ds(c * rows_c, rows_c)
        for v in range(variables):
            high, low = highs[v, rows], lows[v, rows]
            full = dot(
                loy[...],
                jnp.concatenate([column(high[:half], low[:half]), column(high[half:], low[half:])], axis=1),
            )
            for b in range(2):
                lanes = slice(b * nz, (b + 1) * nz)
                to_rows = pl.ds(c * rows_c + b * half, half)
                twice[v, to_rows] = full[:half, lanes]
                fy[v, to_rows] = full[half:, lanes]

    for v in range(variables):
        z_copy(v).wait_recv()

    for v in range(variables):
        theirs = other[v]
        at_low = pltpu.roll(theirs, 2 * EDGE, 1)
        at_low = at_low - at_low.astype(BF16).astype(F32)
        ends = jnp.where((lane >= EDGE) & (lane < 3 * EDGE), at_low, theirs)
        ends = jnp.where((lane >= 3 * EDGE) & (lane < 5 * EDGE), pltpu.roll(theirs, 4 * EDGE, 1), ends).astype(BF16)
        high = highs[v]
        full = dot(jnp.concatenate([high, lows[v]], axis=1), spn[0]) + dot(
            jnp.concatenate([high, ends], axis=1), spn[1]
        )
        tz[v] = full[:, :nz]
        other[v] = full[:, nz:]

    tile = 2 * ny

    @pl.loop(0, rows_all // tile)
    def _(t):
        at = pl.ds(pl.multiple_of(t * tile, tile), tile)
        speed = [vel[d, at] for d in range(3)]
        square = 0.5 * (speed[0] * speed[0] + speed[1] * speed[1] + speed[2] * speed[2])
        heat = (1.0 + 1.0 / GAMMA_LESS) * pre[at] / rho[at] + square
        squares[at] = square
        heats[at] = heat
        gained = pull([other[v, at] for v in range(5)], 2, speed, square, heat)
        for v in range(5):
            tz[v, at] += gained[v]

    def y_fix(c):
        rows = pl.ds(c * rows_c, rows_c)
        for slot in range(2):

            @pl.when(has[2 + slot])
            def _(slot=slot):
                y_copy(1 - slot, c).wait_recv()

        for v in range(variables):
            parts = ([], [])
            for slot in range(2):
                rest, last = yrecv[slot, c, v, 16:24], yrecv[slot, c, v, 24:]
                parts[0].extend([yrecv[slot, c, v, :8], jnp.where(upper | own_rest[2 + slot], rest, 0.0)])
                parts[1].extend(
                    [yrecv[slot, c, v, 8:16], jnp.where(own_rest[2 + slot], last, jnp.where(upper, 0.0, rest))]
                )
            columns = [column(*split(jnp.concatenate(part, axis=0))) for part in parts]
            full = dot(chy[edge[2], edge[3]], jnp.concatenate(columns, axis=1))
            for b in range(2):
                lanes = slice(b * nz, (b + 1) * nz)
                to_rows = pl.ds(c * rows_c + b * half, half)
                twice[v, to_rows] += full[:half, lanes]
                fy[v, to_rows] += full[half:, lanes]

    def take_y(c):
        @pl.loop(0, rows_c // tile)
        def _(t):
            at = pl.ds(pl.multiple_of(c * rows_c + t * tile, tile), tile)
            speed = [vel[d, at] for d in range(3)]
            gain = pull([fy[v, at] for v in range(5)], 1, speed, squares[at], heats[at])
            for v in range(5):
                tz[v, at] += twice[v, at] + gain[v]

    def take_x(c):
        @pl.loop(0, rows_c // tile)
        def _(t):
            at = pl.ds(pl.multiple_of(c * rows_c + t * tile, tile), tile)
            first_line = c * (rows_c // ny) + t * (tile // ny)

            def natural(ref, v):
                return jnp.concatenate(
                    [ref[v, pl.ds(first_line + j, ny, stride=nx)] for j in range(tile // ny)], axis=0
                )

            speed = [vel[d, at] for d in range(3)]
            gain = pull([natural(fx, v) for v in range(5)], 0, speed, squares[at], heats[at])
            for v in range(5):
                total = (tz[v, at] + natural(tx, v)) + gain[v]
                tendency[v, at] = 0.5 * total
                updated[v, at] = adj[v, at] + 0.25 * total

    def combine(c):
        @pl.loop(0, rows_c // tile)
        def _(t):
            at = pl.ds(pl.multiple_of(c * rows_c + t * tile, tile), tile)
            first_line = c * (rows_c // ny) + t * (tile // ny)

            def natural(ref, v):
                return jnp.concatenate(
                    [ref[v, pl.ds(first_line + j, ny, stride=nx)] for j in range(tile // ny)], axis=0
                )

            speed = [vel[d, at] for d in range(3)]
            square, heat = squares[at], heats[at]
            gain = pull_two(
                [natural(fx, v) for v in range(5)], [fy[v, at] for v in range(5)], speed, square, heat
            )
            for v in range(5):
                total = (twice[v, at] + natural(tx, v)) + (tz[v, at] + gain[v])
                tendency[v, at] = 0.5 * total
                updated[v, at] = adj[v, at] + 0.25 * total

    @pl.loop(0, variables)
    def _(v):
        for slot in range(2):

            @pl.when(has[slot])
            def _(slot=slot):
                x_copy(1 - slot, v).wait_recv()

        left = chx[edge[0], edge[1]]
        for q in range(ny // 4):
            columns = [
                column(*split(jnp.concatenate([unpack(slot, v, 2 * q + b) for slot in range(2)], axis=0)))
                for b in range(2)
            ]
            lined = turned[v, q]
            full = dot(left, jnp.concatenate([lined, lined, jnp.concatenate(columns, axis=1)], axis=0))
            for b in range(2):
                lanes = slice(b * nz, (b + 1) * nz)
                to_rows = pl.ds((4 * q + 2 * b) * nx, 2 * nx)
                tx[v, to_rows] = full[: 2 * nx, lanes]
                fx[v, to_rows] = full[2 * nx :, lanes]

    for c in range(chunks):
        y_fix(c)
        combine(c)

    for slot in range(2):
        for c in range(chunks):

            @pl.when(has[2 + slot])
            def _(slot=slot, c=c):
                y_copy(slot, c).wait_send()

        for v in range(variables):

            @pl.when(has[slot])
            def _(slot=slot, v=v):
                x_copy(slot, v).wait_send()

    for v in range(variables):
        z_copy(v).wait_send()


def finish(tendency, updated, tendency_hbm, updated_hbm, sem):
    writes = [
        pltpu.make_async_copy(src, dst, sem.at[k])
        for k, (src, dst) in enumerate(((tendency, tendency_hbm), (updated, updated_hbm)))
    ]
    for write in writes:
        write.start()
    for write in writes:
        write.wait()


def on_device(counts, adjoint, base_density, base_velocity, base_pressure):
    variables, nx, ny, nz = adjoint.shape
    chunks = 3
    rows = nx * ny
    operators = tables(nx, ny, nz)
    field = (variables, rows, nz)
    y_shape = (2, chunks, variables, 8 * RANK, nz)
    x_shape = (2, variables, ny // 2, 2 * RANK, nz)
    dma = pltpu.SemaphoreType.DMA
    hbm = pl.BlockSpec(memory_space=pl.ANY)
    whole = pltpu.VMEM(field, F32)
    whole_low = pltpu.VMEM(field, BF16)
    cells = pltpu.VMEM((rows, nz), F32)
    tendency, updated = pl.pallas_call(
        functools.partial(kernel, counts),
        out_shape=[pltpu.VMEM(field, F32)] * 2,
        in_specs=[hbm] * 10,
        out_specs=[pl.BlockSpec(memory_space=pltpu.VMEM)] * 2,
        scratch_shapes=[
            whole,
            cells,
            pltpu.VMEM((3, rows, nz), F32),
            cells,
            *[pltpu.VMEM(m.shape, BF16) for m in operators],
            whole_low,
            whole_low,
            pltpu.VMEM((variables, ny // 4, 4 * nx, 2 * nz), BF16),
            whole,
            pltpu.VMEM(y_shape, F32),
            pltpu.VMEM(y_shape, F32),
            pltpu.VMEM(x_shape, F32),
            pltpu.VMEM(x_shape, F32),
            whole,
            whole,
            whole,
            whole,
            whole,
            cells,
            cells,
            dma((chunks,)),
            dma((9,)),
            dma((2, chunks)),
            dma((2, chunks)),
            dma((2, variables)),
            dma((2, variables)),
            dma((variables,)),
            dma((variables,)),
        ],
        compiler_params=pltpu.CompilerParams(
            collective_id=0, has_side_effects=True, vmem_limit_bytes=32 << 20
        ),
        name="adjoint_step",
    )(
        *[
            pltpu.with_memory_space_constraint(jnp.asarray(x), pltpu.HBM)
            for x in (
                adjoint.reshape(field),
                base_density.reshape(rows, nz),
                base_velocity.reshape(3, rows, nz),
                base_pressure.reshape(rows, nz),
                *operators,
            )
        ]
    )
    tendency, updated = pl.pallas_call(
        finish,
        out_shape=[jax.ShapeDtypeStruct(field, F32)] * 2,
        in_specs=[pl.BlockSpec(memory_space=pltpu.VMEM)] * 2,
        out_specs=[hbm] * 2,
        scratch_shapes=[dma((2,))],
        compiler_params=pltpu.CompilerParams(vmem_limit_bytes=16 << 20),
        name="finish",
    )(*[pltpu.with_memory_space_constraint(x, pltpu.VMEM) for x in (tendency, updated)])
    return tendency.reshape(adjoint.shape), updated.reshape(adjoint.shape)


def solution(mesh):
    placed = (
        P(None, "gx", "gy", "gz"),
        P("gx", "gy", "gz"),
        P(None, "gx", "gy", "gz"),
        P("gx", "gy", "gz"),
    )
    return jax.shard_map(
        functools.partial(on_device, (mesh.shape["gx"], mesh.shape["gy"])),
        mesh=mesh,
        in_specs=placed,
        out_specs=(P(None, "gx", "gy", "gz"), P(None, "gx", "gy", "gz")),
        check_vma=False,
    )
```

```python
import functools

import jax
import jax.numpy as jnp
import numpy as np
from jax import lax
from jax.experimental import pallas as pl
from jax.experimental.pallas import tpu as pltpu
from jax.sharding import PartitionSpec as P

GAMMA_LESS = 0.4
RATIO = 1.0 / 3.0
COEF_NEAR = 7.0 / 9.0
COEF_FAR = 1.0 / 36.0
RANK = 4
THIN = True
SENT = 24 if THIN else 32
EDGE = 16
F32 = jnp.float32
BF16 = jnp.bfloat16


def derivative(total, periodic):
    eye = np.eye(total)
    if periodic:
        up1, lo1, up2, lo2 = (np.roll(eye, s, axis=1) for s in (1, -1, 2, -2))
    else:
        up1, lo1, up2, lo2 = (np.eye(total, k=s) for s in (1, -1, 2, -2))
    banded = eye + RATIO * (up1 + lo1)
    stencil = COEF_NEAR * (up1 - lo1) + COEF_FAR * (up2 - lo2)
    return -stencil @ np.linalg.inv(banded)


def stacked(matrix, rows, cols):
    return np.vstack([(matrix @ matrix)[rows, cols], -2.0 * matrix[rows, cols]])


def line_factors(block, thin):
    long = derivative(9 * block, False)
    near = derivative(4 * block, False)
    own = slice(4 * block, 5 * block)
    local = stacked(long, own, own)
    sides = []
    for beside, edge in (
        (slice(3 * block, 4 * block), slice(0, block)),
        (slice(5 * block, 6 * block), slice(3 * block, 4 * block)),
    ):
        basis, size, functional = np.linalg.svd(stacked(long, own, beside))
        basis, size, functional = basis[:, :RANK], size[:RANK], functional[:RANK]
        end = (basis, basis.T @ (stacked(near, edge, edge) - local))
        if thin:
            flat = functional.sum(axis=1)
            unseen = np.eye(RANK)[-1] - flat * flat[-1] / (flat @ flat)
            left_out = unseen / size**2
            left_out /= unseen @ left_out
            kept = np.linalg.svd(left_out[None])[2][1:].T
            basis, mixed = np.linalg.qr((basis * size) @ (np.eye(RANK) - np.outer(left_out, unseen)) @ kept)
            sides.append(((basis, mixed @ kept.T @ functional), end))
        else:
            sides.append(((basis, size[:, None] * functional), end))
    return local, sides


def four(matrix):
    high = matrix.astype(np.float32).astype(BF16)
    low = (matrix - high.astype(np.float64)).astype(np.float32).astype(BF16)
    return np.concatenate([high, high, low, low], axis=1)


def direction(block, lines, thin):
    local, sides = line_factors(block, thin)
    eye = np.eye(lines)
    order = [(slice(0, 2), slice(2, 3), slice(2, 3) if thin else slice(3, 4)), (slice(0, 2), slice(2, 3), slice(3, 4))]
    state = np.stack(
        [
            np.stack(
                [
                    four(np.vstack([np.kron(eye, factors[1][part]) for part in order[end]]))
                    for end, factors in enumerate(pair)
                ]
            )
            for pair in ((sides[1][0], sides[0][1]), (sides[0][0], sides[1][1]))
        ]
    )
    whole = four(np.vstack([np.kron(eye, local[:block]), np.kron(eye, local[block:])]))

    def gained(ends):
        return np.vstack(
            [
                np.hstack(
                    [np.kron(eye, side[end][0][half, part]) for side, end in zip(sides, ends) for part in order[end]]
                )
                for half in (slice(0, block), slice(block, None))
            ]
        )

    change = np.stack([np.stack([four(gained((a, b))) for b in range(2)]) for a in range(2)])
    both = np.concatenate([np.broadcast_to(whole, change.shape[:2] + whole.shape), change], axis=-1)
    return state, whole, change, both


def span_table(nz):
    span = derivative(2 * nz, True)
    both = np.hstack([(span @ span)[:nz].T, -2.0 * span[:nz].T])
    high = both.astype(np.float32).astype(BF16)
    low = (both - high.astype(np.float64)).astype(np.float32).astype(BF16)
    first, last = [nz + k for k in range(EDGE)], [2 * nz - EDGE + k for k in range(EDGE)]
    rest = np.zeros((nz - 6 * EDGE, 2 * nz), BF16)
    second = np.concatenate(
        [low[:nz], high[first], high[last], high[first], low[last], low[first], rest, high[last]], axis=0
    )
    return np.stack([np.concatenate([high[:nz], high[:nz]], axis=0), second])


@functools.lru_cache(maxsize=None)
def tables(nx, ny, nz):
    state_y, local_y, change_y, _ = direction(ny, 4, THIN)
    state_x, _, _, both_x = direction(nx, 2, THIN)
    return state_y, local_y, change_y, state_x, both_x, span_table(nz)


def split(value):
    high = value.astype(BF16)
    return high, (value - high.astype(F32)).astype(BF16)


def column(high, low):
    return jnp.concatenate([high, low, high, low], axis=0)


def dot(a, b):
    return jnp.dot(a, b, preferred_element_type=F32)


def pull(first, d, speed, square, enthalpy):
    head = first[1] * speed[0] + first[2] * speed[1] + first[3] * speed[2] + enthalpy * first[4]
    push = GAMMA_LESS * (first[1 + d] + speed[d] * first[4])
    result = [square * push - speed[d] * head]
    for i in range(3):
        term = speed[d] * first[1 + i] - speed[i] * push
        result.append(term + (first[0] + head) if i == d else term)
    result.append(speed[d] * first[4] + push)
    return result


def pull_two(g, k, speed, square, enthalpy):
    head_g = g[1] * speed[0] + g[2] * speed[1] + g[3] * speed[2] + enthalpy * g[4]
    head_k = k[1] * speed[0] + k[2] * speed[1] + k[3] * speed[2] + enthalpy * k[4]
    energy = speed[0] * g[4] + speed[1] * k[4]
    push = GAMMA_LESS * ((g[1] + k[2]) + energy)
    return [
        square * push - (speed[0] * head_g + speed[1] * head_k),
        (speed[0] * (g[1] - push) + speed[1] * k[1]) + (g[0] + head_g),
        (speed[0] * g[2] + speed[1] * (k[2] - push)) + (k[0] + head_k),
        speed[0] * g[3] + speed[1] * k[3] - speed[2] * push,
        energy + push,
    ]


def kernel(
    counts,
    adj_hbm, rho_hbm, vel_hbm, pre_hbm, sty_hbm, loy_hbm, chy_hbm, stx_hbm, chx_hbm, spn_hbm,
    tendency, updated,
    adj, rho, vel, pre, sty, loy, chy, stx, chx, spn,
    highs, lows, turned, other, ysend, yrecv, xsend, xrecv, twice, fy, tx, fx, tz, squares, heats,
    adj_sem, in_sem, ys_sem, yr_sem, xs_sem, xr_sem, zs_sem, zr_sem,
):
    gx, gy, gz = (lax.axis_index(n) for n in ("gx", "gy", "gz"))
    n_gx, n_gy = counts
    variables, rows_all, nz = adj.shape
    chunks = ysend.shape[1]
    rows_c = rows_all // chunks
    half = rows_c // 2
    ny = 16
    nx = rows_all // ny

    pieces = [
        pltpu.make_async_copy(
            adj_hbm.at[:, pl.ds(c * rows_c, rows_c)], adj.at[:, pl.ds(c * rows_c, rows_c)], adj_sem.at[c]
        )
        for c in range(chunks)
    ]
    loads = [
        pltpu.make_async_copy(src, dst, in_sem.at[k])
        for k, (src, dst) in enumerate(
            ((sty_hbm, sty), (stx_hbm, stx), (loy_hbm, loy), (spn_hbm, spn),
             (rho_hbm, rho), (vel_hbm, vel), (pre_hbm, pre), (chx_hbm, chx), (chy_hbm, chy))
        )
    ]
    pieces[0].start()
    loads[0].start()

    has = (gx > 0, gx < n_gx - 1, gy > 0, gy < n_gy - 1)
    edge = tuple(jnp.where(there, 0, 1) for there in has)
    to = ({"gx": gx - 1}, {"gx": gx + 1}, {"gy": gy - 1}, {"gy": gy + 1})
    partner = {"gz": 1 - gz}
    lane = lax.broadcasted_iota(jnp.int32, (rows_all, nz), 1)
    upper = lax.broadcasted_iota(jnp.int32, (8, nz), 0) < 4
    own_rest = tuple(jnp.logical_not(there) if THIN else True for there in has)
    sub = lax.broadcasted_iota(jnp.int32, (8, nz), 0)

    def pack(found):
        ahead = [pltpu.roll(f, 4, 0) if h % 2 else f for h, f in enumerate(found)]
        pairs = [jnp.where(sub < 4, ahead[2 * p], ahead[2 * p + 1]) for p in range(4)]
        thirds = [
            jnp.where(
                sub < 4,
                jnp.where(sub < 2, ahead[g + 1], ahead[g + 3]),
                jnp.where(sub < 6, ahead[g], ahead[g + 2]),
            )
            for g in (0, 4)
        ]
        return pairs + thirds

    def unpack(slot, v, h):
        low = 2 * ((h % 4) // 2) + 4 * (1 - h % 2)
        mine = sub >= 4 if h % 2 else sub < 4
        third = jnp.where((sub >= low) & (sub < low + 2), xrecv[slot, v, 4 + h // 4], 0.0)
        got = jnp.where(mine, xrecv[slot, v, h // 2], third)
        if h % 2:
            got = pltpu.roll(got, 4, 0)
        return jnp.where(own_rest[slot], xrecv[slot, v, h], got)

    barrier = pltpu.get_barrier_semaphore()
    for there, where in zip(has, to):

        @pl.when(there)
        def _(where=where):
            pl.semaphore_signal(barrier, inc=1, device_id=where, device_id_type=pl.DeviceIdType.MESH)

    pl.semaphore_signal(barrier, inc=1, device_id=partner, device_id_type=pl.DeviceIdType.MESH)
    for load in pieces[1:] + loads[1:]:
        load.start()
    neighbours = sum(jnp.where(there, 1, 0) for there in has) + 1

    def remote(src, dst, send, recv, where):
        return pltpu.make_async_remote_copy(
            src_ref=src, dst_ref=dst, send_sem=send, recv_sem=recv,
            device_id=where, device_id_type=pl.DeviceIdType.MESH,
        )

    def y_copy(slot, c):
        return remote(
            ysend.at[slot, c, :, pl.ds(0, SENT)], yrecv.at[1 - slot, c, :, pl.ds(0, SENT)], ys_sem.at[slot, c], yr_sem.at[1 - slot, c], to[2 + slot]
        )

    def x_copy(slot, v):
        return remote(
            xsend.at[slot, v, pl.ds(0, 6)], xrecv.at[1 - slot, v, pl.ds(0, 6)], xs_sem.at[slot, v], xr_sem.at[1 - slot, v], to[slot]
        )

    def z_copy(v):
        return remote(adj_hbm.at[v], other.at[v], zs_sem.at[v], zr_sem.at[v], partner)

    def y_part(c):
        rows = pl.ds(c * rows_c, rows_c)
        left = jnp.concatenate([sty[0, edge[2]], sty[1, edge[3]]], axis=0)
        k = sty.shape[2]
        for v in range(variables):
            high, low = split(adj[v, rows])
            highs[v, rows] = high
            lows[v, rows] = low
            right = jnp.concatenate([column(high[:half], low[:half]), column(high[half:], low[half:])], axis=1)
            full = dot(left, right)
            for slot in range(2):
                pair, rest = full[slot * k : slot * k + 8], full[slot * k + 8 : (slot + 1) * k]
                ysend[slot, c, v, :8] = pair[:, :nz]
                ysend[slot, c, v, 8:16] = pair[:, nz:]
                ysend[slot, c, v, 16:24] = jnp.where(upper | own_rest[2 + slot], rest[:, :nz], rest[:, nz:])
                ysend[slot, c, v, 24:] = rest[:, nz:]

    def y_send(c):
        for slot in range(2):

            @pl.when(has[2 + slot])
            def _(slot=slot):
                y_copy(slot, c).start()

            @pl.when(jnp.logical_not(has[2 + slot]))
            def _(slot=slot):
                yrecv[slot, c] = ysend[slot, c]

    pieces[0].wait()
    loads[0].wait()
    y_part(0)
    for c in range(1, chunks):
        pieces[c].wait()
    loads[1].wait()
    loads[2].wait()

    y_part(1)
    pl.semaphore_wait(barrier, neighbours)
    y_send(0)
    y_send(1)
    for v in range(variables):
        z_copy(v).start()
    @pl.loop(0, variables)
    def _(v):
        found = ([], [])
        left = jnp.concatenate([stx[0, edge[0]], stx[1, edge[1]]], axis=0)
        k = stx.shape[2]
        for q in range(ny // 4):
            halves = []
            for b in range(2):
                lines = [adj[v, pl.ds(4 * q + 2 * b + j, nx, stride=ny)] for j in range(2)]
                halves.append(jnp.concatenate(split(jnp.concatenate(lines, axis=0)), axis=0))
            lined = jnp.concatenate(halves, axis=1)
            turned[v, q] = lined
            full = dot(left, jnp.concatenate([lined, lined], axis=0))
            for b in range(2):
                for slot in range(2):
                    found[slot].append(full[slot * k : (slot + 1) * k, b * nz : (b + 1) * nz])
        for slot in range(2):
            for at, packed in enumerate(pack(found[slot])):
                xsend[slot, v, at] = jnp.where(own_rest[slot], found[slot][at], packed)
            for at in range(6, 8):
                xsend[slot, v, at] = found[slot][at]
        for slot in range(2):

            @pl.when(has[slot])
            def _(slot=slot):
                x_copy(slot, v).start()

            @pl.when(jnp.logical_not(has[slot]))
            def _(slot=slot):
                xrecv[slot, v] = xsend[slot, v]

    for c in range(2, chunks):
        y_part(c)
        y_send(c)

    for load in loads[3:]:
        load.wait()
    for c in range(chunks):
        rows = pl.ds(c * rows_c, rows_c)
        for v in range(variables):
            high, low = highs[v, rows], lows[v, rows]
            full = dot(
                loy[...],
                jnp.concatenate([column(high[:half], low[:half]), column(high[half:], low[half:])], axis=1),
            )
            for b in range(2):
                lanes = slice(b * nz, (b + 1) * nz)
                to_rows = pl.ds(c * rows_c + b * half, half)
                twice[v, to_rows] = full[:half, lanes]
                fy[v, to_rows] = full[half:, lanes]

    for v in range(variables):
        z_copy(v).wait_recv()

    for v in range(variables):
        theirs = other[v]
        at_low = pltpu.roll(theirs, 2 * EDGE, 1)
        at_low = at_low - at_low.astype(BF16).astype(F32)
        ends = jnp.where((lane >= EDGE) & (lane < 3 * EDGE), at_low, theirs)
        ends = jnp.where((lane >= 3 * EDGE) & (lane < 5 * EDGE), pltpu.roll(theirs, 4 * EDGE, 1), ends).astype(BF16)
        high = highs[v]
        full = dot(jnp.concatenate([high, lows[v]], axis=1), spn[0]) + dot(
            jnp.concatenate([high, ends], axis=1), spn[1]
        )
        tz[v] = full[:, :nz]
        other[v] = full[:, nz:]

    tile = 2 * ny

    @pl.loop(0, rows_all // tile)
    def _(t):
        at = pl.ds(pl.multiple_of(t * tile, tile), tile)
        speed = [vel[d, at] for d in range(3)]
        square = 0.5 * (speed[0] * speed[0] + speed[1] * speed[1] + speed[2] * speed[2])
        heat = (1.0 + 1.0 / GAMMA_LESS) * pre[at] / rho[at] + square
        squares[at] = square
        heats[at] = heat
        gained = pull([other[v, at] for v in range(5)], 2, speed, square, heat)
        for v in range(5):
            tz[v, at] += gained[v]

    def y_fix(c):
        rows = pl.ds(c * rows_c, rows_c)
        for slot in range(2):

            @pl.when(has[2 + slot])
            def _(slot=slot):
                y_copy(1 - slot, c).wait_recv()

        for v in range(variables):
            parts = ([], [])
            for slot in range(2):
                rest, last = yrecv[slot, c, v, 16:24], yrecv[slot, c, v, 24:]
                parts[0].extend([yrecv[slot, c, v, :8], jnp.where(upper | own_rest[2 + slot], rest, 0.0)])
                parts[1].extend(
                    [yrecv[slot, c, v, 8:16], jnp.where(own_rest[2 + slot], last, jnp.where(upper, 0.0, rest))]
                )
            columns = [column(*split(jnp.concatenate(part, axis=0))) for part in parts]
            full = dot(chy[edge[2], edge[3]], jnp.concatenate(columns, axis=1))
            for b in range(2):
                lanes = slice(b * nz, (b + 1) * nz)
                to_rows = pl.ds(c * rows_c + b * half, half)
                twice[v, to_rows] += full[:half, lanes]
                fy[v, to_rows] += full[half:, lanes]

    def take_y(c):
        @pl.loop(0, rows_c // tile)
        def _(t):
            at = pl.ds(pl.multiple_of(c * rows_c + t * tile, tile), tile)
            speed = [vel[d, at] for d in range(3)]
            gain = pull([fy[v, at] for v in range(5)], 1, speed, squares[at], heats[at])
            for v in range(5):
                tz[v, at] += twice[v, at] + gain[v]

    def take_x(c):
        @pl.loop(0, rows_c // tile)
        def _(t):
            at = pl.ds(pl.multiple_of(c * rows_c + t * tile, tile), tile)
            first_line = c * (rows_c // ny) + t * (tile // ny)

            def natural(ref, v):
                return jnp.concatenate(
                    [ref[v, pl.ds(first_line + j, ny, stride=nx)] for j in range(tile // ny)], axis=0
                )

            speed = [vel[d, at] for d in range(3)]
            gain = pull([natural(fx, v) for v in range(5)], 0, speed, squares[at], heats[at])
            for v in range(5):
                total = (tz[v, at] + natural(tx, v)) + gain[v]
                tendency[v, at] = 0.5 * total
                updated[v, at] = adj[v, at] + 0.25 * total

    def combine(c):
        @pl.loop(0, rows_c // tile)
        def _(t):
            at = pl.ds(pl.multiple_of(c * rows_c + t * tile, tile), tile)
            first_line = c * (rows_c // ny) + t * (tile // ny)

            def natural(ref, v):
                return jnp.concatenate(
                    [ref[v, pl.ds(first_line + j, ny, stride=nx)] for j in range(tile // ny)], axis=0
                )

            speed = [vel[d, at] for d in range(3)]
            square, heat = squares[at], heats[at]
            gain = pull_two(
                [natural(fx, v) for v in range(5)], [fy[v, at] for v in range(5)], speed, square, heat
            )
            for v in range(5):
                total = (twice[v, at] + natural(tx, v)) + (tz[v, at] + gain[v])
                tendency[v, at] = 0.5 * total
                updated[v, at] = adj[v, at] + 0.25 * total

    y_fix(0)

    @pl.loop(0, variables)
    def _(v):
        for slot in range(2):

            @pl.when(has[slot])
            def _(slot=slot):
                x_copy(1 - slot, v).wait_recv()

        left = chx[edge[0], edge[1]]
        for q in range(ny // 4):
            columns = [
                column(*split(jnp.concatenate([unpack(slot, v, 2 * q + b) for slot in range(2)], axis=0)))
                for b in range(2)
            ]
            lined = turned[v, q]
            full = dot(left, jnp.concatenate([lined, lined, jnp.concatenate(columns, axis=1)], axis=0))
            for b in range(2):
                lanes = slice(b * nz, (b + 1) * nz)
                to_rows = pl.ds((4 * q + 2 * b) * nx, 2 * nx)
                tx[v, to_rows] = full[: 2 * nx, lanes]
                fx[v, to_rows] = full[2 * nx :, lanes]

    combine(0)
    for c in range(1, chunks):
        y_fix(c)
        combine(c)

    for slot in range(2):
        for c in range(chunks):

            @pl.when(has[2 + slot])
            def _(slot=slot, c=c):
                y_copy(slot, c).wait_send()

        for v in range(variables):

            @pl.when(has[slot])
            def _(slot=slot, v=v):
                x_copy(slot, v).wait_send()

    for v in range(variables):
        z_copy(v).wait_send()


def finish(tendency, updated, tendency_hbm, updated_hbm, sem):
    writes = [
        pltpu.make_async_copy(src, dst, sem.at[k])
        for k, (src, dst) in enumerate(((tendency, tendency_hbm), (updated, updated_hbm)))
    ]
    for write in writes:
        write.start()
    for write in writes:
        write.wait()


def on_device(counts, adjoint, base_density, base_velocity, base_pressure):
    variables, nx, ny, nz = adjoint.shape
    chunks = 3
    rows = nx * ny
    operators = tables(nx, ny, nz)
    field = (variables, rows, nz)
    y_shape = (2, chunks, variables, 8 * RANK, nz)
    x_shape = (2, variables, ny // 2, 2 * RANK, nz)
    dma = pltpu.SemaphoreType.DMA
    hbm = pl.BlockSpec(memory_space=pl.ANY)
    whole = pltpu.VMEM(field, F32)
    whole_low = pltpu.VMEM(field, BF16)
    cells = pltpu.VMEM((rows, nz), F32)
    tendency, updated = pl.pallas_call(
        functools.partial(kernel, counts),
        out_shape=[pltpu.VMEM(field, F32)] * 2,
        in_specs=[hbm] * 10,
        out_specs=[pl.BlockSpec(memory_space=pltpu.VMEM)] * 2,
        scratch_shapes=[
            whole,
            cells,
            pltpu.VMEM((3, rows, nz), F32),
            cells,
            *[pltpu.VMEM(m.shape, BF16) for m in operators],
            whole_low,
            whole_low,
            pltpu.VMEM((variables, ny // 4, 4 * nx, 2 * nz), BF16),
            whole,
            pltpu.VMEM(y_shape, F32),
            pltpu.VMEM(y_shape, F32),
            pltpu.VMEM(x_shape, F32),
            pltpu.VMEM(x_shape, F32),
            whole,
            whole,
            whole,
            whole,
            whole,
            cells,
            cells,
            dma((chunks,)),
            dma((9,)),
            dma((2, chunks)),
            dma((2, chunks)),
            dma((2, variables)),
            dma((2, variables)),
            dma((variables,)),
            dma((variables,)),
        ],
        compiler_params=pltpu.CompilerParams(
            collective_id=0, has_side_effects=True, vmem_limit_bytes=32 << 20
        ),
        name="adjoint_step",
    )(
        *[
            pltpu.with_memory_space_constraint(jnp.asarray(x), pltpu.HBM)
            for x in (
                adjoint.reshape(field),
                base_density.reshape(rows, nz),
                base_velocity.reshape(3, rows, nz),
                base_pressure.reshape(rows, nz),
                *operators,
            )
        ]
    )
    tendency, updated = pl.pallas_call(
        finish,
        out_shape=[jax.ShapeDtypeStruct(field, F32)] * 2,
        in_specs=[pl.BlockSpec(memory_space=pltpu.VMEM)] * 2,
        out_specs=[hbm] * 2,
        scratch_shapes=[dma((2,))],
        compiler_params=pltpu.CompilerParams(vmem_limit_bytes=16 << 20),
        name="finish",
    )(*[pltpu.with_memory_space_constraint(x, pltpu.VMEM) for x in (tendency, updated)])
    return tendency.reshape(adjoint.shape), updated.reshape(adjoint.shape)


def solution(mesh):
    placed = (
        P(None, "gx", "gy", "gz"),
        P("gx", "gy", "gz"),
        P(None, "gx", "gy", "gz"),
        P("gx", "gy", "gz"),
    )
    return jax.shard_map(
        functools.partial(on_device, (mesh.shape["gx"], mesh.shape["gy"])),
        mesh=mesh,
        in_specs=placed,
        out_specs=(P(None, "gx", "gy", "gz"), P(None, "gx", "gy", "gz")),
        check_vma=False,
    )
```
